32 devices in a mesh: groups: 2 (over y), seq: 4 (over z), tensor: 2 (over x), sub: 2 (over core).
Axes of the slice: x: 2, y: 2, z: 4, core: 2. Of those that a mesh axis runs over, the one named last changes fastest.
Arguments:
- activations: bfloat16 [4096, 4096], P(('groups', 'seq'), ('tensor', 'sub')), parts along dimension 0, may hold values from -18 to 18
- conv_weight: bfloat16 [512, 4096], P(None, ('tensor', 'sub')), may hold values from -0.25 to 0.25
- query_weight: bfloat16 [4096, 2048], P('seq', ('tensor', 'sub')), may hold values from -0.09375 to 0.09375
- key_weight: bfloat16 [4096, 2048], P('seq', ('tensor', 'sub')), may hold values from -0.09375 to 0.09375
- value_weight: bfloat16 [4096, 2048], P('seq', ('tensor', 'sub')), may hold values from -0.09375 to 0.09375
- segment_for_slot: int32 [16], P('groups'), parts along dimension 0, may hold values from 0 to 7, each once
- book_length: int32 [2], P('groups'), parts along dimension 0, may hold values from 1024 to 2048
Outputs:
- context: bfloat16 [4096, 2048], P(('groups', 'seq'), ('tensor', 'sub')), parts along dimension 0
The draws below stay inside these ranges and needn't reach their ends.
There are 2 independent parts, one for each index of `groups`. The reference program is written for one: setup_inputs(seed, part) draws one part's arguments, and reference() takes and returns one part's arrays. A program takes and returns all parts, laid end to end along the dimension named above; an argument that names none is the same for every part. Nothing has to cross between parts.
Inputs may be any that keep to these rules, and one draw needn't show every extreme that they name: `segment_for_slot`: each segment appears in exactly one slot.
All inputs are finite; a program needn't handle non-finite values.
Results may differ from the reference program's by a relative error of at most 0.012.
The reference program's roundings to bfloat16 on the way (of `compressed` and `weights_low`) count: a program that leaves them out, or rounds other values in their place, can miss the bound.
Values may be sent and summed in bfloat16 or wider, within the bound.
No kernel may reach another device: no remote copies, remote signals or barrier semaphores. Data moves between devices by JAX's collectives and lax.ppermute only.
A program may use at most 64 MiB of HBM per device.

```python
import jax
import jax.numpy as jnp
from jax import lax

D = 4096
HD = 128
HEADS = 16
CG = 128
RATE = 4
SEG = 256
MEM = 64
SEGMENT_SLOTS = 8
TOKENS = 2048


def draw_activations(key, part):
    leading_key = jax.random.fold_in(key, 0)
    normal_part = jax.random.normal(leading_key, (TOKENS, D), jnp.float32)
    return jnp.clip(normal_part, -6.0, 6.0).astype(jnp.bfloat16)


def steps_of(key, shape, cuts, smallest, high):
    factor_of, own = 1.0, jax.random.fold_in(key, 6)
    for dim, parts in cuts:
        steps = jnp.exp(jax.random.uniform(jax.random.fold_in(own, dim), (parts,), jnp.float32, smallest / len(cuts), high / len(cuts)))
        factor_of = factor_of * jnp.repeat(steps, shape[dim] // parts).reshape([-1 if axis == dim else 1 for axis in range(len(shape))])
    return factor_of


def gaussian(stream_key, shape, width, bound, cuts=(), held_as=jnp.bfloat16):
    values = width * jax.random.normal(stream_key, shape, jnp.float32)
    if cuts:
        values = values * steps_of(stream_key, shape, cuts, -0.22, 0.18)
    return jnp.clip(values, -bound, bound).astype(held_as)


def setup_inputs(seed: int = 0, part: int = 0) -> dict:
    streams_of = jax.random.split(jax.random.key(seed), 8)
    part_splits = jax.random.split(jax.random.fold_in(streams_of[7], part), 8)
    activations = draw_activations(jax.random.fold_in(jax.random.fold_in(streams_of[7], part), 71), part)
    conv_weight = gaussian(streams_of[1], (RATE * CG, D), (RATE * CG) ** -0.5, 0.25, ((1, 4),))
    query_weight = gaussian(streams_of[2], (D, HEADS * HD), D ** -0.5, 0.09375, ((0, 4), (1, 4)))
    key_weight = gaussian(streams_of[3], (D, HEADS * HD), D ** -0.5, 0.09375, ((0, 4), (1, 4)))
    value_weight = gaussian(streams_of[4], (D, HEADS * HD), D ** -0.5, 0.09375, ((0, 4), (1, 4)))
    segment_for_slot = jax.random.permutation(part_splits[5], SEGMENT_SLOTS).astype(jnp.int32)
    book_length = jax.random.randint(part_splits[6], (1,), TOKENS // 2, TOKENS + 1).astype(jnp.int32)
    return {"activations": activations, "conv_weight": conv_weight, "query_weight": query_weight, "key_weight": key_weight, "value_weight": value_weight, "segment_for_slot": segment_for_slot, "book_length": book_length}


def reference(activations, conv_weight, query_weight, key_weight, value_weight, segment_for_slot, book_length):
    count_slots = segment_for_slot.shape[0]
    group_count = D // CG
    shaped = activations.astype(jnp.float32).reshape(TOKENS // RATE, RATE, group_count, CG)
    kernel = conv_weight.astype(jnp.float32).reshape(RATE, CG, group_count, CG)
    compressed = jnp.einsum("mtgc,tcgo->mgo", shaped, kernel).reshape(TOKENS // RATE, D).astype(jnp.bfloat16)
    queries = jnp.dot(activations, query_weight, preferred_element_type=jnp.float32).astype(jnp.bfloat16)
    keys_all = jnp.dot(activations, key_weight, preferred_element_type=jnp.float32).astype(jnp.bfloat16)
    values_all = jnp.dot(activations, value_weight, preferred_element_type=jnp.float32).astype(jnp.bfloat16)
    memory_keys = jnp.dot(compressed, key_weight, preferred_element_type=jnp.float32).astype(jnp.bfloat16)
    memory_values = jnp.dot(compressed, value_weight, preferred_element_type=jnp.float32).astype(jnp.bfloat16)
    query_slots = queries.reshape(count_slots, SEG, HEADS, HD)
    key_slots = keys_all.reshape(count_slots, SEG, HEADS, HD)
    value_slots = values_all.reshape(count_slots, SEG, HEADS, HD)
    mem_keys = memory_keys.reshape(count_slots * MEM, HEADS, HD).astype(jnp.float32)
    mem_values = memory_values.reshape(count_slots * MEM, HEADS, HD).astype(jnp.float32)
    mem_segment = jnp.repeat(segment_for_slot, MEM)
    causal = jnp.arange(SEG)[:, None] >= jnp.arange(SEG)[None, :]
    scale_factor = HD ** -0.5

    def one_slot(slot_index):
        query_block = query_slots[slot_index].astype(jnp.float32)
        key_block = key_slots[slot_index].astype(jnp.float32)
        value_block = value_slots[slot_index].astype(jnp.float32)
        segment_here = segment_for_slot[slot_index]
        local_scores = jnp.einsum("snd,tnd->snt", query_block, key_block) * scale_factor
        local_scores = jnp.where(causal[:, None, :], local_scores, -jnp.inf)
        mem_scores = jnp.einsum("snd,knd->snk", query_block, mem_keys) * scale_factor
        allowed = mem_segment < segment_here
        mem_scores = jnp.where(allowed[None, None, :], mem_scores, -jnp.inf)
        scores = jnp.concatenate([local_scores, mem_scores], axis=2)
        row_best = jnp.max(scores, axis=2)
        weights = jnp.exp(scores - row_best[:, :, None])
        denominator = jnp.sum(weights, axis=2)
        weights_low = lax.optimization_barrier(weights.astype(jnp.bfloat16)).astype(jnp.float32)
        merged_values = jnp.concatenate([value_block, mem_values], axis=0)
        weighted_numerator = jnp.einsum("snk,knd->snd", weights_low, merged_values)
        result = weighted_numerator / denominator[:, :, None]
        position = segment_here * SEG + jnp.arange(SEG)
        result = jnp.where((position < book_length[0])[:, None, None], result, 0.0)
        return result.reshape(SEG, HEADS * HD).astype(jnp.bfloat16)

    outputs = lax.map(one_slot, jnp.arange(count_slots))
    return outputs.reshape(TOKENS, HEADS * HD)
```

```python
import jax
import jax.numpy as jnp
from jax import lax
from jax.sharding import PartitionSpec as P

HD = 128
CG = 128
RATE = 4
SEG = 256
MEM = 64
BF = jnp.bfloat16


def swap(value, axis, distance):
    size = lax.axis_size(axis)
    return lax.ppermute(value, axis, [(i, i ^ distance) for i in range(size)])


def after(value, *others):
    return lax.optimization_barrier((value,) + others)[0]


def compress_rows(local_rows, conv_local):
    count_rows, channels = local_rows.shape
    groups = channels // CG
    shaped = local_rows.reshape(count_rows // RATE, RATE, groups, CG)
    kernel = conv_local.reshape(RATE, CG, groups, CG)
    mixed_out = jnp.einsum("mtgc,tcgo->mgo", shaped, kernel, preferred_element_type=jnp.float32)
    return mixed_out.reshape(count_rows // RATE, channels).astype(BF)


def gather_channels(block):
    tensor_size, sub_size = lax.axis_size("tensor"), lax.axis_size("sub")
    tensor_index, sub_index = lax.axis_index("tensor"), lax.axis_index("sub")
    rows, width = block.shape
    whole = jnp.zeros((rows, width * tensor_size * sub_size), block.dtype)
    for kt in range(tensor_size):
        here = swap(block, "tensor", kt) if kt else block
        for ku in range(sub_size):
            piece = swap(here, "sub", ku) if ku else here
            owner = (tensor_index ^ kt) * sub_size + (sub_index ^ ku)
            whole = lax.dynamic_update_slice(whole, piece, (0, owner * width))
    return whole


def attention(queries, keys, values, mem_keys, mem_values, row_segments, mem_segments, length):
    total_rows, width = queries.shape
    heads, slots = width // HD, total_rows // SEG
    shaped_q = queries.reshape(slots, SEG, heads, HD)
    shaped_k = keys.reshape(slots, SEG, heads, HD)
    shaped_v = values.reshape(slots, SEG, heads, HD)
    local = jnp.einsum("asnd,atnd->anst", shaped_q, shaped_k, preferred_element_type=jnp.float32)
    local = local * HD ** (-0.5)
    index = jnp.arange(SEG, dtype=jnp.int32)
    local = jnp.where(index[:, None] >= index[None, :], local, -jnp.inf)
    mk = mem_keys.reshape(-1, heads, HD)
    mv = mem_values.reshape(-1, heads, HD)
    far = jnp.einsum("asnd,knd->ansk", shaped_q, mk, preferred_element_type=jnp.float32)
    far = far * HD ** (-0.5)
    key_segments = jnp.repeat(mem_segments, MEM, total_repeat_length=mk.shape[0])
    allowed = key_segments[None, :] < row_segments[:, None]
    far = jnp.where(allowed[:, None, None, :], far, -jnp.inf)
    best = jnp.maximum(jnp.max(local, axis=3), jnp.max(far, axis=3))[..., None]
    local, far = jnp.exp(local - best), jnp.exp(far - best)
    denominator = jnp.sum(local, axis=3) + jnp.sum(far, axis=3)
    numerator = jnp.einsum(
        "ansk,aknd->ansd", local.astype(BF), shaped_v, preferred_element_type=jnp.float32
    ) + jnp.einsum("ansk,knd->ansd", far.astype(BF), mv, preferred_element_type=jnp.float32)
    result = numerator / denominator[..., None]
    position = row_segments[:, None] * SEG + index[None, :]
    result = jnp.where((position < length)[:, None, :, None], result, 0.0).astype(BF)
    return result.transpose(0, 2, 1, 3).reshape(total_rows, width)


def on_device(
    activations, conv_weight, query_weight, key_weight, value_weight, segment_for_slot, book_length
):
    planes = lax.axis_size("seq")
    plane, group = lax.axis_index("seq"), lax.axis_index("groups")
    parity = plane & 1
    rows, _ = activations.shape
    slots = rows // SEG
    depth, columns = key_weight.shape
    half_depth, half_columns = depth // 2, columns // 2

    partner_rows = swap(activations, "seq", 1)

    def outgoing(weight, target_parity):
        start = (group * half_depth, target_parity * half_columns)
        return lax.dynamic_slice(weight, start, (half_depth, half_columns))

    weights = (key_weight, value_weight, query_weight)
    arrived = [[None] * planes for _ in weights]
    last = {1: partner_rows}
    for which, weight in enumerate(weights):
        pieces = (outgoing(weight, parity), outgoing(weight, 1 - parity))
        for distance in range(1, planes):
            piece = pieces[distance & 1]
            if distance in last:
                piece = after(piece, last[distance])
            near = swap(piece, "seq", distance)
            last[distance] = near
            arrived[which][distance] = (near, swap(near, "groups", 1))

    def whole_weight(which):
        own = lax.dynamic_slice(weights[which], (0, parity * half_columns), (depth, half_columns))
        whole = jnp.zeros((depth * planes, half_columns), BF)
        whole = lax.dynamic_update_slice(whole, own, (plane * depth, 0))
        for distance in range(1, planes):
            start = (plane ^ distance) * depth
            near, far = arrived[which][distance]
            whole = lax.dynamic_update_slice(whole, near, (start + group * half_depth, 0))
            whole = lax.dynamic_update_slice(whole, far, (start + (1 - group) * half_depth, 0))
        return whole

    own_block = jnp.concatenate([activations, compress_rows(activations, conv_weight)], axis=0)
    partner_block = jnp.concatenate([partner_rows, compress_rows(partner_rows, conv_weight)], axis=0)
    own_all, partner_all = gather_channels(own_block), gather_channels(partner_block)

    def product(which, source):
        return jnp.dot(source, whole[which], preferred_element_type=jnp.float32).astype(BF)

    whole = [whole_weight(which) for which in range(3)]
    k_own, k_partner = product(0, own_all), product(0, partner_all)
    v_own, v_partner = product(1, own_all), product(1, partner_all)
    q_own, q_partner = product(2, own_all[:rows]), product(2, partner_all[:rows])

    mem = [jnp.concatenate([a[rows:], b[rows:]], axis=0) for a, b in ((k_own, k_partner), (v_own, v_partner))]
    mem_keys = jnp.concatenate([mem[0]] + [swap(mem[0], "seq", d) for d in range(2, planes, 2)], axis=0)
    mem_values = jnp.concatenate([mem[1]] + [swap(mem[1], "seq", d) for d in range(2, planes, 2)], axis=0)
    by_plane = segment_for_slot.reshape(planes, slots)
    mem_segments = jnp.concatenate([lax.dynamic_index_in_dim(by_plane, plane ^ d, 0, keepdims=False) for d in range(planes)])
    context = attention(
        jnp.concatenate([q_own, q_partner], axis=0),
        jnp.concatenate([k_own[:rows], k_partner[:rows]], axis=0),
        jnp.concatenate([v_own[:rows], v_partner[:rows]], axis=0),
        mem_keys,
        mem_values,
        mem_segments[: 2 * slots],
        mem_segments,
        book_length[0],
    )
    mine, theirs = context[:rows], swap(context[rows:], "seq", 1)
    return jnp.where(
        parity == 0,
        jnp.concatenate([mine, theirs], axis=1),
        jnp.concatenate([theirs, mine], axis=1),
    )


def solution(mesh):
    placed = (
        P(("groups", "seq"), ("tensor", "sub")),
        P(None, ("tensor", "sub")),
        P("seq", ("tensor", "sub")),
        P("seq", ("tensor", "sub")),
        P("seq", ("tensor", "sub")),
        P("groups"),
        P("groups"),
    )
    return jax.shard_map(
        on_device,
        mesh=mesh,
        in_specs=placed,
        out_specs=P(("groups", "seq"), ("tensor", "sub")),
        check_vma=False,
    )
```

```python
import functools
import math

import jax
import jax.numpy as jnp
from jax import lax
from jax.experimental import pallas as pl
from jax.experimental.pallas import tpu as pltpu
from jax.sharding import PartitionSpec as P

HD = 128
CG = 128
RATE = 4
SEG = 256
MEM = 64
BF = jnp.bfloat16


def cost(microseconds):
    return pl.CostEstimate(flops=int(microseconds * 1.0e9), bytes_accessed=1000, transcendentals=0)
F32 = jnp.float32
ANY = pl.BlockSpec(memory_space=pl.ANY)
SMEM = pl.BlockSpec(memory_space=pltpu.SMEM)
VMEM = pl.BlockSpec(memory_space=pltpu.VMEM)


EARLY = 2


def swap(value, axis, distance, label):
    size = lax.axis_size(axis)
    with jax.named_scope("L_" + label):
        return lax.ppermute(value, axis, [(i, i ^ distance) for i in range(size)])


def after(value, *others):
    return lax.optimization_barrier((value,) + others)[0]


def run_copies(copies):
    for copy in copies:
        copy.start()
    for copy in copies:
        copy.wait()


def aligned(index, size):
    return pl.ds(pl.multiple_of(index * size, size), size)


def split_kernel(wk, wv, wq, kv_same, kv_other, q_same, q_other, sems):
    group, parity = lax.axis_index("groups"), lax.axis_index("seq") & 1
    half, width = q_same.shape
    rows = aligned(group, half)
    copies = []
    for target, kv, q in ((parity, kv_same, q_same), (1 - parity, kv_other, q_other)):
        columns = aligned(target, width)
        for source, dest in (
            (wk, kv.at[:, 0:width]),
            (wv, kv.at[:, width : 2 * width]),
            (wq, q),
        ):
            copies.append(pltpu.make_async_copy(source.at[rows, columns], dest, sems.at[len(copies)]))
    run_copies(copies)


def split_weights(wk, wv, wq):
    depth, columns = wk.shape
    half, width = depth // 2, columns // 2
    shapes = [(half, 2 * width), (half, 2 * width), (half, width), (half, width)]
    return pl.pallas_call(
        split_kernel,
        out_shape=[jax.ShapeDtypeStruct(s, BF) for s in shapes],
        in_specs=[ANY] * 3,
        out_specs=[VMEM] * 4,
        scratch_shapes=[pltpu.SemaphoreType.DMA((6,))],
        cost_estimate=cost(2),
        name="split_weights",
    )(wk, wv, wq)


def compress_kernel(own_ref, partner_ref, w_ref, out_ref):
    rows, channels = own_ref.shape
    count = rows // RATE
    row = lax.broadcasted_iota(jnp.int32, (count, rows), 0)
    column = lax.broadcasted_iota(jnp.int32, (count, rows), 1)
    taps = []
    for t in range(RATE):
        pick = (column == row * RATE + t).astype(BF)
        pair = [jnp.dot(pick, ref[...], preferred_element_type=F32).astype(BF) for ref in (own_ref, partner_ref)]
        taps.append(jnp.concatenate(pair, axis=0))
    for g in range(channels // CG):
        columns = slice(g * CG, (g + 1) * CG)
        total = jnp.zeros((2 * count, CG), F32)
        for t in range(RATE):
            weight = w_ref[t * CG : (t + 1) * CG, columns]
            total += jnp.dot(taps[t][:, columns], weight, preferred_element_type=F32)
        out_ref[:, columns] = total.astype(BF)


def compress(own, partner, conv_weight):
    count, channels = own.shape
    return pl.pallas_call(
        compress_kernel,
        out_shape=jax.ShapeDtypeStruct((2 * count // RATE, channels), BF),
        in_specs=[VMEM, VMEM, VMEM],
        out_specs=VMEM,
        cost_estimate=cost(5),
        name="compress",
    )(own, partner, conv_weight)


def weight_copies(planes, buffer, sems, owns, nears, fars):
    plane, group = lax.axis_index("seq"), lax.axis_index("groups")
    depth = owns[0][0].shape[0]
    half = depth // 2
    copies = []
    for ref, columns, place in owns:
        dest = buffer.at[aligned(plane, depth), place]
        copies.append(pltpu.make_async_copy(ref.at[:, columns], dest, sems.at[len(copies)]))
    for distance in range(1, planes):
        first = (plane ^ distance) * 2
        for ref, side in ((nears[distance - 1], group), (fars[distance - 1], 1 - group)):
            dest = buffer.at[aligned(first + side, half), :]
            copies.append(pltpu.make_async_copy(ref, dest, sems.at[len(copies)]))
    return copies


def block_owner(index, tensor_size, sub_size):
    tensor, sub = lax.axis_index("tensor"), lax.axis_index("sub")
    return (tensor ^ (index // sub_size)) * sub_size + (sub ^ (index % sub_size))


def project_kernel(planes, tensor_size, sub_size, counts, *refs):
    blocks, others = tensor_size * sub_size, planes - 1
    wk, wv = refs[:2]
    nears, fars, refs = refs[2 : 2 + others], refs[2 + others : 2 + 2 * others], refs[2 + 2 * others :]
    groups = [refs[i * blocks : (i + 1) * blocks] for i in range(len(counts))]
    out, xbuf, wbuf, acc, xsem, wsem = refs[len(counts) * blocks :]
    width = wbuf.shape[1] // 2
    columns = aligned(lax.axis_index("seq") & 1, width)
    owns = [(wk, columns, slice(0, width)), (wv, columns, slice(width, 2 * width))]
    wcopies = weight_copies(planes, wbuf, wsem, owns, nears, fars)
    for copy in wcopies:
        copy.start()
    xcopies = []
    for j in range(blocks):
        row = 0
        for i, count in enumerate(counts):
            dest = xbuf.at[j, row : row + count, :]
            xcopies.append(pltpu.make_async_copy(groups[i][j], dest, xsem.at[len(xcopies)]))
            xcopies[-1].start()
            row += count
    for copy in wcopies:
        copy.wait()
    product_loop(tensor_size, sub_size, counts, xcopies, xbuf, wbuf, acc, out)


def product_loop(tensor_size, sub_size, counts, xcopies, xbuf, wbuf, acc, out):
    blocks, chunk = xbuf.shape[0], xbuf.shape[2]
    for j in range(blocks):
        weight = aligned(block_owner(j, tensor_size, sub_size), chunk)
        row = 0
        for i, count in enumerate(counts):
            rows = slice(row, row + count)
            row += count
            xcopies[j * len(counts) + i].wait()
            part = jnp.dot(xbuf[j, rows, :], wbuf[weight, :], preferred_element_type=F32)
            if j:
                part += acc[rows, :]
            if j < blocks - 1:
                acc[rows, :] = part
            else:
                out[rows, :] = part.astype(BF)


def project(planes, tensor_size, sub_size, wk, wv, nears, fars, groups, name):
    depth, columns = wk.shape
    blocks = tensor_size * sub_size
    counts = [g[0].shape[0] for g in groups]
    chunk, total = groups[0][0].shape[1], sum(counts)
    operands = [wk, wv, *nears, *fars] + [block for g in groups for block in g]
    return pl.pallas_call(
        functools.partial(project_kernel, planes, tensor_size, sub_size, counts),
        out_shape=jax.ShapeDtypeStruct((total, columns), BF),
        in_specs=[ANY] * len(operands),
        out_specs=VMEM,
        scratch_shapes=[
            pltpu.VMEM((blocks, total, chunk), BF),
            pltpu.VMEM((depth * planes, columns), BF),
            pltpu.VMEM((total, columns), F32),
            pltpu.SemaphoreType.DMA((len(groups) * blocks,)),
            pltpu.SemaphoreType.DMA((2 + 2 * (planes - 1),)),
        ],
        compiler_params=pltpu.CompilerParams(vmem_limit_bytes=62 << 20),
        cost_estimate=cost(2 + total // 128),
        name=name,
    )(*operands)


def attend_kernel(side, planes, tensor_size, sub_size, *refs):
    blocks, others = tensor_size * sub_size, planes - 1
    segments, length, wq = refs[:3]
    refs = refs[3:]
    nears, fars, refs = refs[:others], refs[others : 2 * others], refs[2 * others :]
    xs, refs = refs[:blocks], refs[blocks:]
    kv_tok, refs = refs[0], refs[1:]
    mems, refs = refs[: planes // 2], refs[planes // 2 :]
    out, xbuf, wbuf, acc, qbuf, kvbuf, membuf, xsem, wsem, ksem = refs
    plane = lax.axis_index("seq")
    width = wbuf.shape[1]
    rows_here = out.shape[0]
    slots = rows_here // SEG
    owns = [(wq, aligned(plane & 1, width), slice(0, width))]
    wcopies = weight_copies(planes, wbuf, wsem, owns, nears, fars)
    xcopies = [pltpu.make_async_copy(xs[j], xbuf.at[j], xsem.at[j]) for j in range(blocks)]
    kcopies = [pltpu.make_async_copy(kv_tok.at[pl.ds(side * rows_here, rows_here), :], kvbuf, ksem.at[0])]
    count = mems[0].shape[0]
    for i, mem in enumerate(mems):
        kcopies.append(pltpu.make_async_copy(mem, membuf.at[pl.ds(i * count, count), :], ksem.at[1 + i]))
    for copy in wcopies + xcopies + kcopies:
        copy.start()
    per_plane = count // 2
    mem_total = membuf.shape[0]
    column = lax.broadcasted_iota(jnp.int32, (1, mem_total), 1)
    owner = jnp.zeros((1, mem_total), jnp.int32)
    for distance in range(planes):
        for i in range(slots):
            start = distance * per_plane + i * MEM
            here = (column >= start) & (column < start + MEM)
            owner = jnp.where(here, segments[(plane ^ distance) * slots + i], owner)
    row = lax.broadcasted_iota(jnp.int32, (SEG, SEG), 0)
    causal = row >= lax.broadcasted_iota(jnp.int32, (SEG, SEG), 1)
    position = lax.broadcasted_iota(jnp.int32, (SEG, HD), 0)
    contract = (((1,), (1,)), ((), ()))
    scale = HD ** (-0.5) * math.log2(math.e)
    for copy in wcopies:
        copy.wait()
    product_loop(tensor_size, sub_size, [rows_here], xcopies, xbuf, wbuf, acc, qbuf)
    for copy in kcopies:
        copy.wait()
    for a in range(slots):
        rows = slice(a * SEG, (a + 1) * SEG)
        segment = segments[(plane ^ side) * slots + a]
        allowed = owner < segment
        valid = position + segment * SEG < length[0]
        for h in range(width // HD):
            ks, vs = slice(h * HD, (h + 1) * HD), slice(width + h * HD, width + (h + 1) * HD)
            query = qbuf[rows, ks]
            near = lax.dot_general(query, kvbuf[rows, ks], contract, preferred_element_type=F32)
            far = lax.dot_general(query, membuf[:, ks], contract, preferred_element_type=F32)
            near = jnp.where(causal, near * scale, -jnp.inf)
            far = jnp.where(allowed, far * scale, -jnp.inf)
            best = jnp.maximum(
                jnp.max(near, axis=1, keepdims=True), jnp.max(far, axis=1, keepdims=True)
            )
            near, far = jnp.exp2(near - best), jnp.exp2(far - best)
            denominator = jnp.sum(near, axis=1, keepdims=True) + jnp.sum(far, axis=1, keepdims=True)
            numerator = jnp.dot(near.astype(BF), kvbuf[rows, vs], preferred_element_type=F32)
            numerator += jnp.dot(far.astype(BF), membuf[:, vs], preferred_element_type=F32)
            out[rows, ks] = jnp.where(valid, numerator / denominator, 0.0).astype(BF)


def attend(side, planes, tensor_size, sub_size, segments, length, wq, nears, fars, xs, kv_tok, mems):
    depth, columns = wq.shape
    width = columns // 2
    rows, chunk = xs[0].shape
    blocks = tensor_size * sub_size
    mem_total = len(mems) * mems[0].shape[0]
    operands = [segments, length, wq, *nears, *fars, *xs, kv_tok, *mems]
    return pl.pallas_call(
        functools.partial(attend_kernel, side, planes, tensor_size, sub_size),
        out_shape=jax.ShapeDtypeStruct((rows, width), BF),
        in_specs=[SMEM, SMEM] + [ANY] * (len(operands) - 2),
        out_specs=VMEM,
        scratch_shapes=[
            pltpu.VMEM((blocks, rows, chunk), BF),
            pltpu.VMEM((depth * planes, width), BF),
            pltpu.VMEM((rows, width), F32),
            pltpu.VMEM((rows, width), BF),
            pltpu.VMEM((rows, 2 * width), BF),
            pltpu.VMEM((mem_total, 2 * width), BF),
            pltpu.SemaphoreType.DMA((blocks,)),
            pltpu.SemaphoreType.DMA((1 + 2 * (planes - 1),)),
            pltpu.SemaphoreType.DMA((1 + len(mems),)),
        ],
        compiler_params=pltpu.CompilerParams(vmem_limit_bytes=62 << 20),
        cost_estimate=cost(8),
        name="attend",
    )(*operands)


def on_device(
    activations, conv_weight, query_weight, key_weight, value_weight, segment_for_slot, book_length
):
    planes, tensor_size, sub_size = (lax.axis_size(name) for name in ("seq", "tensor", "sub"))
    parity = lax.axis_index("seq") & 1

    kv_same, kv_other, q_same, q_other = split_weights(key_weight, value_weight, query_weight)

    def across(block, label):
        return {f"{label}x{k}": (block, "tensor", k) for k in range(1, tensor_size)}

    def within(block, label):
        return {f"{label}c{k}": (block, "sub", k) for k in range(1, sub_size)}

    def distant(distances, name):
        same, other = {"kv": (kv_same, kv_other), "q": (q_same, q_other)}[name]
        return {f"{name}{d}": (other if d & 1 else same, "seq", d) for d in distances}

    def relayed(distances, name):
        return {f"y{name}{d}": (got[f"{name}{d}"], "groups", 1) for d in distances}

    got = {}

    def stage(sends, *computed):
        held = tuple(got[key] for key in fresh)
        new = {}
        for key, (value, axis, distance) in sends.items():
            new[key] = swap(after(value, *held), axis, distance, key)
        ended = lax.optimization_barrier(tuple(new.values()) + computed)
        got.update(zip(new, ended))
        fresh[:] = list(new)
        return ended[len(new) :]

    fresh = []
    every = range(1, planes)
    first = [2] if planes > 2 else []
    second = [d for d in every if d not in first]
    stage(
        {"Xz": (activations, "seq", 1)}
        | across(activations, "A")
        | within(activations, "A0")
        | distant(first, "kv")
    )
    partner = got["Xz"]
    sends = across(partner, "B") | within(partner, "B0") | distant(second, "kv") | relayed(first, "kv")
    for k in range(1, tensor_size):
        sends |= within(got[f"Ax{k}"], f"A{k}")
    (both,) = stage(sends, compress(activations, partner, conv_weight))
    sends = across(both, "C") | within(both, "C0") | distant(every, "q") | relayed(second, "kv")
    for k in range(1, tensor_size):
        sends |= within(got[f"Bx{k}"], f"B{k}")
    stage(sends)
    sends = relayed(every, "q")
    for k in range(1, tensor_size):
        sends |= within(got[f"Cx{k}"], f"C{k}")
    held = tuple(got[key] for key in fresh)
    for key, (value, axis, distance) in sends.items():
        got[key] = swap(after(value, *held), axis, distance, key)

    def pieces(block, label):
        whole = []
        for k in range(tensor_size):
            whole.append(got[f"{label}x{k}"] if k else block)
            whole += [got[f"{label}{k}c{u}"] for u in range(1, sub_size)]
        return whole

    own_pieces, partner_pieces = pieces(activations, "A"), pieces(partner, "B")
    compressed_pieces = pieces(both, "C")
    near_kv, far_kv = ({d: got[f"{y}kv{d}"] for d in every} for y in ("", "y"))
    near_q, far_q = ({d: got[f"{y}q{d}"] for d in every} for y in ("", "y"))

    distances = range(1, planes)
    sizes = (planes, tensor_size, sub_size)
    kv_parts = ([near_kv[d] for d in distances], [far_kv[d] for d in distances])
    kv_mem = project(*sizes, key_weight, value_weight, *kv_parts, (compressed_pieces,), "project_memory")
    mems = [kv_mem] + [swap(kv_mem, "seq", d, f"m{d}") for d in range(2, planes, 2)]
    kv_tok = project(
        *sizes, after(key_weight, kv_mem), value_weight, *kv_parts, (own_pieces, partner_pieces), "project_tokens"
    )
    shared = (
        query_weight,
        [near_q[d] for d in distances],
        [far_q[d] for d in distances],
    )
    theirs = attend(1, *sizes, segment_for_slot, book_length, *shared, partner_pieces, kv_tok, mems)
    returned = swap(theirs, "seq", 1, "ctx")
    mine = attend(0, *sizes, segment_for_slot, book_length, *shared, own_pieces, kv_tok, mems)
    width = mine.shape[1]
    result = jnp.concatenate([mine, mine], axis=1)
    return lax.dynamic_update_slice(result, returned, (0, (1 - parity) * width))


def solution(mesh):
    placed = (
        P(("groups", "seq"), ("tensor", "sub")),
        P(None, ("tensor", "sub")),
        P("seq", ("tensor", "sub")),
        P("seq", ("tensor", "sub")),
        P("seq", ("tensor", "sub")),
        P("groups"),
        P("groups"),
    )
    return jax.shard_map(
        on_device,
        mesh=mesh,
        in_specs=placed,
        out_specs=P(("groups", "seq"), ("tensor", "sub")),
        check_vma=False,
    )
```

```python
import functools
import math

import jax
import jax.numpy as jnp
from jax import lax
from jax.experimental import pallas as pl
from jax.experimental.pallas import tpu as pltpu
from jax.sharding import PartitionSpec as P

HD = 128
CG = 128
RATE = 4
SEG = 256
MEM = 64
BF = jnp.bfloat16


def cost(microseconds):
    return pl.CostEstimate(flops=int(microseconds * 1.0e9), bytes_accessed=1000, transcendentals=0)
F32 = jnp.float32
ANY = pl.BlockSpec(memory_space=pl.ANY)
MEMORY_LIMIT, TOKENS_LIMIT, VMEM_LIMIT = 58 << 20, 40 << 20, 40 << 20
SMEM = pl.BlockSpec(memory_space=pltpu.SMEM)
VMEM = pl.BlockSpec(memory_space=pltpu.VMEM)


EARLY = 2


def swap(value, axis, distance, label):
    size = lax.axis_size(axis)
    with jax.named_scope("L_" + label):
        return lax.ppermute(value, axis, [(i, i ^ distance) for i in range(size)])


def after(value, *others):
    return lax.optimization_barrier((value,) + others)[0]


def resident(value):
    return pltpu.with_memory_space_constraint(value, pltpu.VMEM)


def run_copies(copies):
    for copy in copies:
        copy.start()
    for copy in copies:
        copy.wait()


def aligned(index, size):
    return pl.ds(pl.multiple_of(index * size, size), size)


def split_kernel(wk, wv, wq, kv_same, kv_other, q_same, q_other, q_whole, sems):
    group, parity = lax.axis_index("groups"), lax.axis_index("seq") & 1
    half, width = q_same.shape
    rows = aligned(group, half)
    copies = []
    for target, kv, q in ((parity, kv_same, q_same), (1 - parity, kv_other, q_other)):
        columns = aligned(target, width)
        for source, dest in ((wk, kv.at[:, 0:width]), (wv, kv.at[:, width : 2 * width]), (wq, q)):
            copies.append(pltpu.make_async_copy(source.at[rows, columns], dest, sems.at[len(copies)]))
    source = wq.at[:, aligned(1 - parity, width)]
    copies.append(pltpu.make_async_copy(source, q_whole, sems.at[len(copies)]))
    run_copies(copies)


def split_weights(wk, wv, wq):
    depth, columns = wk.shape
    half, width = depth // 2, columns // 2
    shapes = [(half, 2 * width), (half, 2 * width), (half, width), (half, width), (depth, width)]
    return pl.pallas_call(
        split_kernel,
        out_shape=[jax.ShapeDtypeStruct(s, BF) for s in shapes],
        in_specs=[ANY] * 3,
        out_specs=[VMEM] * 5,
        scratch_shapes=[pltpu.SemaphoreType.DMA((7,))],
        cost_estimate=cost(2),
        name="split_weights",
    )(wk, wv, wq)


def compress_kernel(own_ref, partner_ref, w_ref, out_ref):
    rows, channels = own_ref.shape
    count = rows // RATE
    row = lax.broadcasted_iota(jnp.int32, (count, rows), 0)
    column = lax.broadcasted_iota(jnp.int32, (count, rows), 1)
    taps = []
    for t in range(RATE):
        pick = (column == row * RATE + t).astype(BF)
        pair = [jnp.dot(pick, ref[...], preferred_element_type=F32).astype(BF) for ref in (own_ref, partner_ref)]
        taps.append(jnp.concatenate(pair, axis=0))
    for g in range(channels // CG):
        columns = slice(g * CG, (g + 1) * CG)
        total = jnp.zeros((2 * count, CG), F32)
        for t in range(RATE):
            weight = w_ref[t * CG : (t + 1) * CG, columns]
            total += jnp.dot(taps[t][:, columns], weight, preferred_element_type=F32)
        out_ref[:, columns] = total.astype(BF)


def compress(own, partner, conv_weight):
    count, channels = own.shape
    return pl.pallas_call(
        compress_kernel,
        out_shape=jax.ShapeDtypeStruct((2 * count // RATE, channels), BF),
        in_specs=[VMEM, VMEM, VMEM],
        out_specs=VMEM,
        cost_estimate=cost(5),
        name="compress",
    )(own, partner, conv_weight)


def weight_copies(planes, buffer, sems, owns, nears, fars):
    plane, group = lax.axis_index("seq"), lax.axis_index("groups")
    depth = owns[0][0].shape[0]
    half = depth // 2
    pieces = [(ref.at[:, columns], aligned(plane, depth), place) for ref, columns, place in owns]
    fars = iter(fars)
    for distance, near in enumerate(nears, 1):
        if near.shape[0] == depth:
            pieces.append((near, aligned(plane ^ distance, depth), slice(None)))
        else:
            first = (plane ^ distance) * 2
            pieces.append((near, aligned(first + group, half), slice(None)))
            pieces.append((next(fars), aligned(first + 1 - group, half), slice(None)))
    copies = []
    for ref, rows, place in pieces:
        copies.append(pltpu.make_async_copy(ref, buffer.at[rows, place], sems.at[len(copies)]))
    return copies


def block_owner(index, tensor_size, sub_size):
    tensor, sub = lax.axis_index("tensor"), lax.axis_index("sub")
    return (tensor ^ (index // sub_size)) * sub_size + (sub ^ (index % sub_size))


def memory_kernel(planes, tensor_size, sub_size, *refs):
    blocks, others = tensor_size * sub_size, planes - 1
    wk, wv = refs[:2]
    nears, fars, refs = refs[2 : 2 + others], refs[2 + others : 2 + 2 * others], refs[2 + 2 * others :]
    pieces, (out, wbuf, xbuf, acc, xsem, wsem) = refs[:blocks], refs[blocks:]
    width = wbuf.shape[1] // 2
    columns = aligned(lax.axis_index("seq") & 1, width)
    owns = [(wk, columns, slice(0, width)), (wv, columns, slice(width, 2 * width))]
    wcopies = weight_copies(planes, wbuf, wsem, owns, nears, fars)
    xcopies = [pltpu.make_async_copy(pieces[j], xbuf.at[j], xsem.at[j]) for j in range(blocks)]
    run_copies(wcopies + xcopies)
    product_loop(tensor_size, sub_size, xbuf, pl.ds(0, out.shape[0]), wbuf, acc, out)


def product_loop(tensor_size, sub_size, xbuf, rows, wbuf, acc, out):
    blocks, chunk = xbuf.shape[0], xbuf.shape[2]
    for j in range(blocks):
        weight = aligned(block_owner(j, tensor_size, sub_size), chunk)
        part = jnp.dot(xbuf[j, rows, :], wbuf[weight, :], preferred_element_type=F32)
        if j:
            part += acc[...]
        if j < blocks - 1:
            acc[...] = part
        else:
            out[...] = part.astype(BF)


def project_memory(planes, tensor_size, sub_size, wk, wv, nears, fars, pieces):
    depth, columns = wk.shape
    blocks, (rows, chunk) = len(pieces), pieces[0].shape
    operands = [wk, wv, *nears, *fars, *pieces]
    return pl.pallas_call(
        functools.partial(memory_kernel, planes, tensor_size, sub_size),
        out_shape=[jax.ShapeDtypeStruct((rows, columns), BF), pltpu.VMEM((depth * planes, columns), BF)],
        in_specs=[ANY] * len(operands),
        out_specs=[VMEM, VMEM],
        scratch_shapes=[
            pltpu.VMEM((blocks, rows, chunk), BF),
            pltpu.VMEM((rows, columns), F32),
            pltpu.SemaphoreType.DMA((blocks,)),
            pltpu.SemaphoreType.DMA((2 + 2 * (planes - 1),)),
        ],
        compiler_params=pltpu.CompilerParams(vmem_limit_bytes=MEMORY_LIMIT),
        cost_estimate=cost(4),
        name="project_memory",
    )(*operands)


def tokens_kernel(tensor_size, sub_size, *refs):
    blocks = tensor_size * sub_size
    pieces, (wbuf, out, xbuf, acc, sems) = refs[: 2 * blocks], refs[2 * blocks :]
    rows, chunk = pieces[0].shape
    copies = []
    for j in range(blocks):
        for side in range(2):
            dest = xbuf.at[j, pl.ds(side * rows, rows), :]
            copies.append(pltpu.make_async_copy(pieces[side * blocks + j], dest, sems.at[len(copies)]))
    for copy in copies:
        copy.start()
    for j in range(blocks):
        weight = aligned(block_owner(j, tensor_size, sub_size), chunk)
        for side in range(2):
            copies[2 * j + side].wait()
            here = slice(side * rows, (side + 1) * rows)
            part = jnp.dot(xbuf[j, here, :], wbuf[weight, :], preferred_element_type=F32)
            if j:
                part += acc[here, :]
            if j < blocks - 1:
                acc[here, :] = part
            else:
                out[here, :] = part.astype(BF)


def project_tokens(tensor_size, sub_size, own, partner, weights):
    blocks, (rows, chunk), columns = len(own), own[0].shape, weights.shape[1]
    return pl.pallas_call(
        functools.partial(tokens_kernel, tensor_size, sub_size),
        out_shape=[pltpu.VMEM((2 * rows, columns), BF), pltpu.VMEM((blocks, 2 * rows, chunk), BF)],
        in_specs=[ANY] * (2 * blocks) + [VMEM],
        out_specs=[VMEM, VMEM],
        scratch_shapes=[pltpu.VMEM((2 * rows, columns), F32), pltpu.SemaphoreType.DMA((2 * blocks,))],
        compiler_params=pltpu.CompilerParams(vmem_limit_bytes=TOKENS_LIMIT),
        cost_estimate=cost(6),
        name="project_tokens",
    )(*own, *partner, resident(weights))


def attend_kernel(side, planes, tensor_size, sub_size, halves, *refs):
    segments, length, wq = refs[:3]
    refs = refs[3:]
    nears, fars, refs = refs[: planes - 1], refs[planes - 1 : planes - 1 + halves], refs[planes - 1 + halves :]
    xbuf, kvbuf, refs = refs[0], refs[1], refs[2:]
    mems, refs = refs[: planes // 2], refs[planes // 2 :]
    out, wbuf, acc, qbuf, membuf, obuf, wsem, ksem = refs
    plane = lax.axis_index("seq")
    rows_here, width = qbuf.shape
    slots = rows_here // SEG
    owns = [(wq, aligned(plane & 1, width), slice(0, width))]
    wcopies = weight_copies(planes, wbuf, wsem, owns, nears, fars)
    count = mems[0].shape[0]
    kcopies = []
    for i, mem in enumerate(mems):
        kcopies.append(pltpu.make_async_copy(mem, membuf.at[pl.ds(i * count, count), :], ksem.at[1 + i]))
    for copy in wcopies + kcopies:
        copy.start()
    per_plane = count // 2
    mem_total = membuf.shape[0]
    column = lax.broadcasted_iota(jnp.int32, (1, mem_total), 1)
    owner = jnp.zeros((1, mem_total), jnp.int32)
    for distance in range(planes):
        for i in range(slots):
            start = distance * per_plane + i * MEM
            inside = (column >= start) & (column < start + MEM)
            owner = jnp.where(inside, segments[(plane ^ distance) * slots + i], owner)
    row = lax.broadcasted_iota(jnp.int32, (SEG, SEG), 0)
    causal = row >= lax.broadcasted_iota(jnp.int32, (SEG, SEG), 1)
    position = lax.broadcasted_iota(jnp.int32, (SEG, HD), 0)
    contract = (((1,), (1,)), ((), ()))
    scale = HD ** (-0.5) * math.log2(math.e)
    for copy in wcopies:
        copy.wait()
    product_loop(tensor_size, sub_size, xbuf, pl.ds(side * rows_here, rows_here), wbuf, acc, qbuf)
    for copy in kcopies:
        copy.wait()
    for a in range(slots):
        rows = slice(a * SEG, (a + 1) * SEG)
        kvrows = slice(side * rows_here + a * SEG, side * rows_here + (a + 1) * SEG)
        segment = segments[(plane ^ side) * slots + a]
        allowed = owner < segment
        valid = position + segment * SEG < length[0]
        for h in range(width // HD):
            ks, vs = slice(h * HD, (h + 1) * HD), slice(width + h * HD, width + (h + 1) * HD)
            query = qbuf[rows, ks]
            near = lax.dot_general(query, kvbuf[kvrows, ks], contract, preferred_element_type=F32)
            far = lax.dot_general(query, membuf[:, ks], contract, preferred_element_type=F32)
            near = jnp.where(causal, near * scale, -jnp.inf)
            far = jnp.where(allowed, far * scale, -jnp.inf)
            best = jnp.maximum(
                jnp.max(near, axis=1, keepdims=True), jnp.max(far, axis=1, keepdims=True)
            )
            near, far = jnp.exp2(near - best), jnp.exp2(far - best)
            denominator = jnp.sum(near, axis=1, keepdims=True) + jnp.sum(far, axis=1, keepdims=True)
            numerator = jnp.dot(near.astype(BF), kvbuf[kvrows, vs], preferred_element_type=F32)
            numerator += jnp.dot(far.astype(BF), membuf[:, vs], preferred_element_type=F32)
            obuf[rows, ks] = jnp.where(valid, numerator / denominator, 0.0).astype(BF)
    dest = out if side else out.at[:, aligned(plane & 1, width)]
    copy = pltpu.make_async_copy(obuf, dest, ksem.at[0])
    copy.start()
    copy.wait()


def attend(side, planes, tensor_size, sub_size, segments, length, wq, nears, fars, held, kv_tok, mems):
    depth, columns = wq.shape
    rows, width = held.shape[1] // 2, columns // 2
    mem_total = len(mems) * mems[0].shape[0]
    operands = [segments, length, wq, *nears, *fars, resident(held), resident(kv_tok), *mems]
    return pl.pallas_call(
        functools.partial(attend_kernel, side, planes, tensor_size, sub_size, len(fars)),
        out_shape=jax.ShapeDtypeStruct((rows, width if side else 2 * width), BF),
        in_specs=[SMEM, SMEM] + [ANY] * (len(operands) - 4 - len(mems)) + [VMEM] * 2 + [ANY] * len(mems),
        out_specs=ANY,
        scratch_shapes=[
            pltpu.VMEM((depth * planes, width), BF),
            pltpu.VMEM((rows, width), F32),
            pltpu.VMEM((rows, width), BF),
            pltpu.VMEM((mem_total, 2 * width), BF),
            pltpu.VMEM((rows, width), BF),
            pltpu.SemaphoreType.DMA((1 + len(nears) + len(fars),)),
            pltpu.SemaphoreType.DMA((1 + len(mems),)),
        ],
        compiler_params=pltpu.CompilerParams(vmem_limit_bytes=VMEM_LIMIT),
        cost_estimate=cost(6),
        name="attend",
    )(*operands)


def on_device(
    activations, conv_weight, query_weight, key_weight, value_weight, segment_for_slot, book_length
):
    planes, tensor_size, sub_size = (lax.axis_size(name) for name in ("seq", "tensor", "sub"))
    parity = lax.axis_index("seq") & 1

    kv_same, kv_other, q_same, q_other, q_whole = split_weights(key_weight, value_weight, query_weight)

    def across(block, label):
        return {f"{label}x{k}": (block, "tensor", k) for k in range(1, tensor_size)}

    def within(block, label):
        return {f"{label}c{k}": (block, "sub", k) for k in range(1, sub_size)}

    def distant(distances, name):
        same, other = {"kv": (kv_same, kv_other), "q": (q_same, q_other)}[name]
        return {f"{name}{d}": (other if d & 1 else same, "seq", d) for d in distances}

    def relayed(distances, name):
        return {f"y{name}{d}": (got[f"{name}{d}"], "groups", 1) for d in distances}

    got = {}

    def stage(sends, *computed):
        held = tuple(got[key] for key in fresh)
        new = {}
        for key, (value, axis, distance) in sends.items():
            new[key] = swap(after(value, *held), axis, distance, key)
        ended = lax.optimization_barrier(tuple(new.values()) + computed)
        got.update(zip(new, ended))
        fresh[:] = list(new)
        return ended[len(new) :]

    fresh = []
    every = range(1, planes)
    first = [2] if planes > 2 else []
    second = [d for d in every if d not in first]
    stage(
        {"Xz": (activations, "seq", 1)}
        | across(activations, "A")
        | within(activations, "A0")
        | distant(first, "kv")
    )
    partner = got["Xz"]
    sends = across(partner, "B") | within(partner, "B0") | distant(second, "kv") | relayed(first, "kv")
    for k in range(1, tensor_size):
        sends |= within(got[f"Ax{k}"], f"A{k}")
    (both,) = stage(sends, compress(activations, partner, conv_weight))
    far_planes = range(2, planes)
    stage(distant(far_planes, "q") | relayed(second, "kv") | across(both, "C"))
    sends = within(both, "C0") | {"q1": (q_whole, "seq", 1)} | relayed(far_planes, "q")
    for label in ("C", "B"):
        for k in range(1, tensor_size):
            sends |= within(got[f"{label}x{k}"], f"{label}{k}")
    before = tuple(got[key] for key in fresh)
    for key, (value, axis, distance) in sends.items():
        got[key] = swap(after(value, *before), axis, distance, key)

    def pieces(block, label):
        whole = []
        for k in range(tensor_size):
            whole.append(got[f"{label}x{k}"] if k else block)
            whole += [got[f"{label}{k}c{u}"] for u in range(1, sub_size)]
        return whole

    own_pieces, partner_pieces = pieces(activations, "A"), pieces(partner, "B")
    compressed_pieces = pieces(both, "C")
    sizes = (planes, tensor_size, sub_size)
    kv_parts = ([got[f"kv{d}"] for d in every], [got[f"ykv{d}"] for d in every])
    kv_mem, kv_held = project_memory(*sizes, key_weight, value_weight, *kv_parts, compressed_pieces)
    mems = [kv_mem] + [swap(kv_mem, "seq", d, f"m{d}") for d in range(2, planes, 2)]
    kv_tok, held = project_tokens(tensor_size, sub_size, own_pieces, partner_pieces, kv_held)
    q_parts = ([got[f"q{d}"] for d in every], [got[f"yq{d}"] for d in far_planes])
    shared = (book_length, query_weight, *q_parts, held, kv_tok, mems)
    theirs = attend(1, *sizes, segment_for_slot, *shared)
    returned = swap(theirs, "seq", 1, "ctx")
    mine = attend(0, *sizes, after(segment_for_slot, theirs), *shared)
    return lax.dynamic_update_slice(mine, returned, (0, (1 - parity) * theirs.shape[1]))


def solution(mesh):
    placed = (
        P(("groups", "seq"), ("tensor", "sub")),
        P(None, ("tensor", "sub")),
        P("seq", ("tensor", "sub")),
        P("seq", ("tensor", "sub")),
        P("seq", ("tensor", "sub")),
        P("groups"),
        P("groups"),
    )
    return jax.shard_map(
        on_device,
        mesh=mesh,
        in_specs=placed,
        out_specs=P(("groups", "seq"), ("tensor", "sub")),
        check_vma=False,
    )
```

```python
import functools
import math

import jax
import jax.numpy as jnp
from jax import lax
from jax.experimental import pallas as pl
from jax.experimental.pallas import tpu as pltpu
from jax.sharding import PartitionSpec as P

HD = 128
CG = 128
RATE = 4
SEG = 256
MEM = 64
BF = jnp.bfloat16


def cost(microseconds):
    return pl.CostEstimate(flops=int(microseconds * 1.0e9), bytes_accessed=1000, transcendentals=0)
F32 = jnp.float32
ANY = pl.BlockSpec(memory_space=pl.ANY)
MEMORY_LIMIT, TOKENS_LIMIT, VMEM_LIMIT = 48 << 20, 38 << 20, 26 << 20
SMEM = pl.BlockSpec(memory_space=pltpu.SMEM)
VMEM = pl.BlockSpec(memory_space=pltpu.VMEM)


EARLY = 2


def swap(value, axis, distance, label):
    size = lax.axis_size(axis)
    with jax.named_scope("L_" + label):
        return lax.ppermute(value, axis, [(i, i ^ distance) for i in range(size)])


def after(value, *others):
    return lax.optimization_barrier((value,) + others)[0]


def resident(value):
    return pltpu.with_memory_space_constraint(value, pltpu.VMEM)


def run_copies(copies):
    for copy in copies:
        copy.start()
    for copy in copies:
        copy.wait()


def aligned(index, size):
    return pl.ds(pl.multiple_of(index * size, size), size)


def split_kernel(wk, wv, wq, kv_same, kv_other, q_same, q_other, q_whole, sems):
    group, parity = lax.axis_index("groups"), lax.axis_index("seq") & 1
    half, width = q_same.shape
    rows = aligned(group, half)
    copies = []
    for target, kv, q in ((parity, kv_same, q_same), (1 - parity, kv_other, q_other)):
        columns = aligned(target, width)
        for source, dest in ((wk, kv.at[:, 0:width]), (wv, kv.at[:, width : 2 * width]), (wq, q)):
            copies.append(pltpu.make_async_copy(source.at[rows, columns], dest, sems.at[len(copies)]))
    source = wq.at[:, aligned(1 - parity, width)]
    copies.append(pltpu.make_async_copy(source, q_whole, sems.at[len(copies)]))
    run_copies(copies)


def split_weights(wk, wv, wq):
    depth, columns = wk.shape
    half, width = depth // 2, columns // 2
    shapes = [(half, 2 * width), (half, 2 * width), (half, width), (half, width), (depth, width)]
    return pl.pallas_call(
        split_kernel,
        out_shape=[jax.ShapeDtypeStruct(s, BF) for s in shapes],
        in_specs=[ANY] * 3,
        out_specs=[VMEM] * 5,
        scratch_shapes=[pltpu.SemaphoreType.DMA((7,))],
        cost_estimate=cost(2),
        name="split_weights",
    )(wk, wv, wq)


def compress_kernel(own_ref, partner_ref, w_ref, out_ref):
    rows, channels = own_ref.shape
    count = rows // RATE
    row = lax.broadcasted_iota(jnp.int32, (count, rows), 0)
    column = lax.broadcasted_iota(jnp.int32, (count, rows), 1)
    taps = []
    for t in range(RATE):
        pick = (column == row * RATE + t).astype(BF)
        pair = [jnp.dot(pick, ref[...], preferred_element_type=F32).astype(BF) for ref in (own_ref, partner_ref)]
        taps.append(jnp.concatenate(pair, axis=0))
    for g in range(channels // CG):
        columns = slice(g * CG, (g + 1) * CG)
        total = jnp.zeros((2 * count, CG), F32)
        for t in range(RATE):
            weight = w_ref[t * CG : (t + 1) * CG, columns]
            total += jnp.dot(taps[t][:, columns], weight, preferred_element_type=F32)
        out_ref[:, columns] = total.astype(BF)


def compress(own, partner, conv_weight):
    count, channels = own.shape
    return pl.pallas_call(
        compress_kernel,
        out_shape=jax.ShapeDtypeStruct((2 * count // RATE, channels), BF),
        in_specs=[VMEM, VMEM, VMEM],
        out_specs=VMEM,
        cost_estimate=cost(5),
        name="compress",
    )(own, partner, conv_weight)


def weight_copies(buffer, sems, owns, nears, fars, far_order):
    plane, group = lax.axis_index("seq"), lax.axis_index("groups")
    depth = owns[0][0].shape[0]
    half = depth // 2
    pieces = [(ref.at[:, columns], aligned(plane, depth), place) for ref, columns, place in owns]
    for distance, near in enumerate(nears, 1):
        if near.shape[0] == depth:
            pieces.append((near, aligned(plane ^ distance, depth), slice(None)))
        else:
            pieces.append((near, aligned((plane ^ distance) * 2 + group, half), slice(None)))
    order = iter(far_order)
    for far in fars:
        for i in range(far.shape[0] // half):
            place = aligned((plane ^ next(order)) * 2 + 1 - group, half)
            pieces.append((far.at[pl.ds(i * half, half), :], place, slice(None)))
    copies = []
    for ref, rows, place in pieces:
        copies.append(pltpu.make_async_copy(ref, buffer.at[rows, place], sems.at[len(copies)]))
    return copies


def block_owner(index, tensor_size, sub_size):
    tensor, sub = lax.axis_index("tensor"), lax.axis_index("sub")
    return (tensor ^ (index // sub_size)) * sub_size + (sub ^ (index % sub_size))


def memory_kernel(planes, tensor_size, sub_size, far_order, halves, *refs):
    blocks = tensor_size * sub_size
    wk, wv = refs[:2]
    nears, fars, refs = refs[2 : planes + 1], refs[planes + 1 : planes + 1 + halves], refs[planes + 1 + halves :]
    pieces, (out, wbuf, xbuf, acc, xsem, wsem) = refs[:blocks], refs[blocks:]
    width = wbuf.shape[1] // 2
    columns = aligned(lax.axis_index("seq") & 1, width)
    owns = [(wk, columns, slice(0, width)), (wv, columns, slice(width, 2 * width))]
    wcopies = weight_copies(wbuf, wsem, owns, nears, fars, far_order)
    xcopies = [pltpu.make_async_copy(pieces[j], xbuf.at[j], xsem.at[j]) for j in range(blocks)]
    for copy in wcopies + xcopies:
        copy.start()
    for copy in wcopies:
        copy.wait()
    product_loop(tensor_size, sub_size, xbuf, wbuf, acc, out, xcopies)


def product_loop(tensor_size, sub_size, xbuf, wbuf, acc, out, waits=()):
    blocks, chunk = xbuf.shape[0], xbuf.shape[2]
    for j in range(blocks):
        if waits:
            waits[j].wait()
        weight = aligned(block_owner(j, tensor_size, sub_size), chunk)
        part = jnp.dot(xbuf[j], wbuf[weight, :], preferred_element_type=F32)
        if j:
            part += acc[...]
        if j < blocks - 1:
            acc[...] = part
        else:
            out[...] = part.astype(BF)


def project_memory(planes, tensor_size, sub_size, wk, wv, nears, fars, far_order, pieces):
    depth, columns = wk.shape
    blocks, (rows, chunk) = len(pieces), pieces[0].shape
    operands = [wk, wv, *nears, *fars, *pieces]
    return pl.pallas_call(
        functools.partial(memory_kernel, planes, tensor_size, sub_size, far_order, len(fars)),
        out_shape=[jax.ShapeDtypeStruct((rows, columns), BF), pltpu.VMEM((depth * planes, columns), BF)],
        in_specs=[ANY] * len(operands),
        out_specs=[VMEM, VMEM],
        scratch_shapes=[
            pltpu.VMEM((blocks, rows, chunk), BF),
            pltpu.VMEM((rows, columns), F32),
            pltpu.SemaphoreType.DMA((blocks,)),
            pltpu.SemaphoreType.DMA((2 + 2 * (planes - 1),)),
        ],
        compiler_params=pltpu.CompilerParams(vmem_limit_bytes=MEMORY_LIMIT),
        cost_estimate=cost(4),
        name="project_memory",
    )(*operands)


def tokens_kernel(tensor_size, sub_size, *refs):
    blocks = tensor_size * sub_size
    pieces, (wbuf, out, xbuf, acc, sems) = refs[: 2 * blocks], refs[2 * blocks :]
    rows, chunk = pieces[0].shape
    copies = []
    for j in range(blocks):
        for side in range(2):
            dest = xbuf.at[j, pl.ds(side * rows, rows), :]
            copies.append(pltpu.make_async_copy(pieces[side * blocks + j], dest, sems.at[len(copies)]))
    for copy in copies:
        copy.start()
    for j in range(blocks):
        weight = aligned(block_owner(j, tensor_size, sub_size), chunk)
        for side in range(2):
            copies[2 * j + side].wait()
            here = slice(side * rows, (side + 1) * rows)
            part = jnp.dot(xbuf[j, here, :], wbuf[weight, :], preferred_element_type=F32)
            if j:
                part += acc[here, :]
            if j < blocks - 1:
                acc[here, :] = part
            else:
                out[here, :] = part.astype(BF)


def project_tokens(tensor_size, sub_size, own, partner, weights):
    blocks, (rows, chunk), columns = len(own), own[0].shape, weights.shape[1]
    return pl.pallas_call(
        functools.partial(tokens_kernel, tensor_size, sub_size),
        out_shape=[pltpu.VMEM((2 * rows, columns), BF), pltpu.VMEM((blocks, 2 * rows, chunk), BF)],
        in_specs=[ANY] * (2 * blocks) + [VMEM],
        out_specs=[VMEM, VMEM],
        scratch_shapes=[pltpu.VMEM((2 * rows, columns), F32), pltpu.SemaphoreType.DMA((2 * blocks,))],
        compiler_params=pltpu.CompilerParams(vmem_limit_bytes=TOKENS_LIMIT),
        cost_estimate=cost(6),
        name="project_tokens",
    )(*own, *partner, resident(weights))


SCALE = HD ** (-0.5) * math.log2(math.e)
CONTRACT = (((1,), (1,)), ((), ()))


def local_kernel(side, planes, tensor_size, sub_size, far_order, halves, *refs):
    refs = refs[1:]
    if halves is None:
        wbuf, xbuf, kvbuf, queries, sums, largest, totals = refs
    else:
        wq, refs = refs[0], refs[1:]
        nears, fars, refs = refs[: planes - 1], refs[planes - 1 : planes - 1 + halves], refs[planes - 1 + halves :]
        xbuf, kvbuf, queries, sums, largest, totals, wbuf, wsem = refs
        owns = [(wq, aligned(lax.axis_index("seq") & 1, wbuf.shape[1]), slice(None))]
        run_copies(weight_copies(wbuf, wsem, owns, nears, fars, far_order))
    rows_here, width = queries.shape
    here = pl.ds(side * rows_here, rows_here)
    product_loop(tensor_size, sub_size, xbuf.at[:, here, :], wbuf, sums, queries)
    row = lax.broadcasted_iota(jnp.int32, (SEG, SEG), 0)
    causal = row >= lax.broadcasted_iota(jnp.int32, (SEG, SEG), 1)
    for a in range(rows_here // SEG):
        rows = slice(a * SEG, (a + 1) * SEG)
        kvrows = slice(side * rows_here + a * SEG, side * rows_here + (a + 1) * SEG)
        for h in range(width // HD):
            ks, vs = slice(h * HD, (h + 1) * HD), slice(width + h * HD, width + (h + 1) * HD)
            scores = lax.dot_general(queries[rows, ks], kvbuf[kvrows, ks], CONTRACT, preferred_element_type=F32)
            scores = jnp.where(causal, scores * SCALE, -jnp.inf)
            best = jnp.max(scores, axis=1, keepdims=True)
            weights = jnp.exp2(scores - best)
            largest[rows, ks] = jnp.broadcast_to(best, (SEG, HD))
            totals[rows, ks] = jnp.broadcast_to(jnp.sum(weights, axis=1, keepdims=True), (SEG, HD))
            sums[rows, ks] = jnp.dot(weights.astype(BF), kvbuf[kvrows, vs], preferred_element_type=F32)


def attend_local(side, planes, tensor_size, sub_size, turn, weight, far_order, held, kv_tok):
    rows, width = held.shape[1] // 2, kv_tok.shape[1] // 2
    state = [pltpu.VMEM((rows, width), BF)] + [pltpu.VMEM((rows, width), F32)] * 3
    scratch, halves = [], None
    if isinstance(weight, tuple):
        wq, nears, fars = weight
        operands, halves = [wq, *nears, *fars], len(fars)
        specs = [ANY] * len(operands)
        state.append(pltpu.VMEM((wq.shape[0] * planes, width), BF))
        scratch = [pltpu.SemaphoreType.DMA((planes + len(far_order),))]
    else:
        operands, specs = [resident(weight)], [VMEM]
    return pl.pallas_call(
        functools.partial(local_kernel, side, planes, tensor_size, sub_size, far_order, halves),
        out_shape=state,
        in_specs=[SMEM] + specs + [VMEM] * 2,
        out_specs=[VMEM] * len(state),
        scratch_shapes=scratch,
        compiler_params=pltpu.CompilerParams(vmem_limit_bytes=VMEM_LIMIT),
        cost_estimate=cost(4),
        name="attend_local",
    )(turn, *operands, resident(held), resident(kv_tok))


def far_kernel(side, planes, segments, length, queries, sums, largest, totals, *refs):
    mems, (out, membuf, obuf, sems) = refs[: planes // 2], refs[planes // 2 :]
    plane = lax.axis_index("seq")
    rows_here, width = obuf.shape
    slots = rows_here // SEG
    count = mems[0].shape[0]
    copies = []
    for i, mem in enumerate(mems):
        copies.append(pltpu.make_async_copy(mem, membuf.at[pl.ds(i * count, count), :], sems.at[1 + i]))
        copies[-1].start()
    per_plane = count // 2
    mem_total = membuf.shape[0]
    column = lax.broadcasted_iota(jnp.int32, (1, mem_total), 1)
    owner = jnp.zeros((1, mem_total), jnp.int32)
    for distance in range(planes):
        for i in range(slots):
            start = distance * per_plane + i * MEM
            inside = (column >= start) & (column < start + MEM)
            owner = jnp.where(inside, segments[(plane ^ distance) * slots + i], owner)
    position = lax.broadcasted_iota(jnp.int32, (SEG, HD), 0)
    for copy in copies:
        copy.wait()
    for a in range(slots):
        rows = slice(a * SEG, (a + 1) * SEG)
        segment = segments[(plane ^ side) * slots + a]
        allowed = owner < segment
        valid = position + segment * SEG < length[0]
        for h in range(width // HD):
            ks, vs = slice(h * HD, (h + 1) * HD), slice(width + h * HD, width + (h + 1) * HD)
            scores = lax.dot_general(queries[rows, ks], membuf[:, ks], CONTRACT, preferred_element_type=F32)
            scores = jnp.where(allowed, scores * SCALE, -jnp.inf)
            before = largest[rows, ks]
            best = jnp.maximum(before[:, :1], jnp.max(scores, axis=1, keepdims=True))
            weights = jnp.exp2(scores - best)
            factor = jnp.exp2(before - best)
            denominator = totals[rows, ks] * factor + jnp.sum(weights, axis=1, keepdims=True)
            numerator = sums[rows, ks] * factor
            numerator += jnp.dot(weights.astype(BF), membuf[:, vs], preferred_element_type=F32)
            obuf[rows, ks] = jnp.where(valid, numerator / denominator, 0.0).astype(BF)
    dest = out if side else out.at[:, aligned(plane & 1, width)]
    copy = pltpu.make_async_copy(obuf, dest, sems.at[0])
    copy.start()
    copy.wait()


def attend(side, planes, segments, length, state, mems):
    rows, width = state[0].shape
    mem_total = len(mems) * mems[0].shape[0]
    operands = [segments, length, *(resident(value) for value in state), *mems]
    return pl.pallas_call(
        functools.partial(far_kernel, side, planes),
        out_shape=jax.ShapeDtypeStruct((rows, width if side else 2 * width), BF),
        in_specs=[SMEM, SMEM] + [VMEM] * len(state) + [ANY] * len(mems),
        out_specs=ANY,
        scratch_shapes=[
            pltpu.VMEM((mem_total, 2 * width), BF),
            pltpu.VMEM((rows, width), BF),
            pltpu.SemaphoreType.DMA((1 + len(mems),)),
        ],
        compiler_params=pltpu.CompilerParams(vmem_limit_bytes=VMEM_LIMIT),
        cost_estimate=cost(4),
        name="attend",
    )(*operands)


def on_device(
    activations, conv_weight, query_weight, key_weight, value_weight, segment_for_slot, book_length
):
    planes, tensor_size, sub_size = (lax.axis_size(name) for name in ("seq", "tensor", "sub"))
    parity = lax.axis_index("seq") & 1

    kv_same, kv_other, q_same, q_other, q_whole = split_weights(key_weight, value_weight, query_weight)

    def across(block, label):
        return {f"{label}x{k}": (block, "tensor", k) for k in range(1, tensor_size)}

    def within(block, label):
        return {f"{label}c{k}": (block, "sub", k) for k in range(1, sub_size)}

    def distant(distances, name):
        same, other = {"kv": (kv_same, kv_other), "q": (q_same, q_other)}[name]
        return {f"{name}{d}": (other if d & 1 else same, "seq", d) for d in distances}

    def relayed(distances, name):
        return {f"y{name}{d}": (got[f"{name}{d}"], "groups", 1) for d in distances}

    got = {}

    def stage(sends, *computed):
        held = tuple(got[key] for key in fresh)
        new = {}
        for key, (value, axis, distance) in sends.items():
            new[key] = swap(after(value, *held), axis, distance, key)
        ended = lax.optimization_barrier(tuple(new.values()) + computed)
        got.update(zip(new, ended))
        fresh[:] = list(new)
        return ended[len(new) :]

    fresh = []
    every = range(1, planes)
    first = [2] if planes > 2 else []
    second = [d for d in every if d not in first]
    stage(
        {"Xz": (activations, "seq", 1)}
        | across(activations, "A")
        | within(activations, "A0")
        | distant(first, "kv")
    )
    partner = got["Xz"]
    sends = across(partner, "B") | within(partner, "B0") | distant(second, "kv") | relayed(first, "kv")
    for k in range(1, tensor_size):
        sends |= within(got[f"Ax{k}"], f"A{k}")
    (both,) = stage(sends, compress(activations, partner, conv_weight))
    far_planes = range(2, planes)
    second_kv = jnp.concatenate([got[f"kv{d}"] for d in second], axis=0)
    stage(
        distant(far_planes, "q")
        | {"q1": (q_whole, "seq", 1), "ykv": (second_kv, "groups", 1)}
        | across(both, "C")
    )
    sends = within(both, "C0") | relayed(far_planes, "q")
    for label in ("C", "B"):
        for k in range(1, tensor_size):
            sends |= within(got[f"{label}x{k}"], f"{label}{k}")
    before = tuple(got[key] for key in fresh)
    for key, (value, axis, distance) in sends.items():
        held = before if axis == "groups" else ()
        got[key] = swap(after(value, *held), axis, distance, key)

    def pieces(block, label):
        whole = []
        for k in range(tensor_size):
            whole.append(got[f"{label}x{k}"] if k else block)
            whole += [got[f"{label}{k}c{u}"] for u in range(1, sub_size)]
        return whole

    own_pieces, partner_pieces = pieces(activations, "A"), pieces(partner, "B")
    compressed_pieces = pieces(both, "C")
    sizes = (planes, tensor_size, sub_size)
    kv_parts = ([got[f"kv{d}"] for d in every], [got[f"ykv{d}"] for d in first] + [got["ykv"]], first + second)
    kv_mem, kv_held = project_memory(*sizes, key_weight, value_weight, *kv_parts, compressed_pieces)
    mems = [kv_mem] + [swap(kv_mem, "seq", d, f"m{d}") for d in range(2, planes, 2)]
    kv_tok, held = project_tokens(tensor_size, sub_size, own_pieces, partner_pieces, kv_held)
    q_parts = (query_weight, [got[f"q{d}"] for d in every], [got[f"yq{d}"] for d in far_planes])
    q_order = list(far_planes)
    *state, q_held = attend_local(1, *sizes, segment_for_slot, q_parts, q_order, held, kv_tok)
    theirs = attend(1, planes, segment_for_slot, book_length, state, mems)
    returned = swap(theirs, "seq", 1, "ctx")
    turn = after(segment_for_slot, theirs)
    state = attend_local(0, *sizes, turn, q_held, q_order, held, kv_tok)
    mine = attend(0, planes, segment_for_slot, book_length, state, mems)
    return lax.dynamic_update_slice(mine, returned, (0, (1 - parity) * theirs.shape[1]))


def solution(mesh):
    placed = (
        P(("groups", "seq"), ("tensor", "sub")),
        P(None, ("tensor", "sub")),
        P("seq", ("tensor", "sub")),
        P("seq", ("tensor", "sub")),
        P("seq", ("tensor", "sub")),
        P("groups"),
        P("groups"),
    )
    return jax.shard_map(
        on_device,
        mesh=mesh,
        in_specs=placed,
        out_specs=P(("groups", "seq"), ("tensor", "sub")),
        check_vma=False,
    )
```

```python
import functools
import math

import jax
import jax.numpy as jnp
from jax import lax
from jax.experimental import pallas as pl
from jax.experimental.pallas import tpu as pltpu
from jax.sharding import PartitionSpec as P

HD = 128
CG = 128
RATE = 4
SEG = 256
MEM = 64
BF = jnp.bfloat16


def cost(microseconds):
    return pl.CostEstimate(flops=int(microseconds * 1.0e9), bytes_accessed=1000, transcendentals=0)
F32 = jnp.float32
ANY = pl.BlockSpec(memory_space=pl.ANY)
MEMORY_LIMIT, TOKENS_LIMIT, VMEM_LIMIT = 48 << 20, 38 << 20, 26 << 20
SMEM = pl.BlockSpec(memory_space=pltpu.SMEM)
VMEM = pl.BlockSpec(memory_space=pltpu.VMEM)


EARLY = 2


def swap(value, axis, distance, label):
    size = lax.axis_size(axis)
    with jax.named_scope("L_" + label):
        return lax.ppermute(value, axis, [(i, i ^ distance) for i in range(size)])


def after(value, *others):
    return lax.optimization_barrier((value,) + others)[0]


def resident(value):
    return pltpu.with_memory_space_constraint(value, pltpu.VMEM)


def run_copies(copies):
    for copy in copies:
        copy.start()
    for copy in copies:
        copy.wait()


def aligned(index, size):
    return pl.ds(pl.multiple_of(index * size, size), size)


def split_kernel(wk, wv, wq, kv_same, kv_other, q_same, q_other, q_whole, sems):
    group, parity = lax.axis_index("groups"), lax.axis_index("seq") & 1
    half, width = q_same.shape
    rows = aligned(group, half)
    copies = []
    for target, kv, q in ((parity, kv_same, q_same), (1 - parity, kv_other, q_other)):
        columns = aligned(target, width)
        for source, dest in ((wk, kv.at[:, 0:width]), (wv, kv.at[:, width : 2 * width]), (wq, q)):
            copies.append(pltpu.make_async_copy(source.at[rows, columns], dest, sems.at[len(copies)]))
    source = wq.at[:, aligned(1 - parity, width)]
    copies.append(pltpu.make_async_copy(source, q_whole, sems.at[len(copies)]))
    run_copies(copies)


def split_weights(wk, wv, wq):
    depth, columns = wk.shape
    half, width = depth // 2, columns // 2
    shapes = [(half, 2 * width), (half, 2 * width), (half, width), (half, width), (depth, width)]
    return pl.pallas_call(
        split_kernel,
        out_shape=[jax.ShapeDtypeStruct(s, BF) for s in shapes],
        in_specs=[ANY] * 3,
        out_specs=[VMEM] * 5,
        scratch_shapes=[pltpu.SemaphoreType.DMA((7,))],
        cost_estimate=cost(2),
        name="split_weights",
    )(wk, wv, wq)


def compress_kernel(own_ref, partner_ref, w_ref, out_ref):
    rows, channels = own_ref.shape
    count = rows // RATE
    row = lax.broadcasted_iota(jnp.int32, (count, rows), 0)
    column = lax.broadcasted_iota(jnp.int32, (count, rows), 1)
    taps = []
    for t in range(RATE):
        pick = (column == row * RATE + t).astype(BF)
        pair = [jnp.dot(pick, ref[...], preferred_element_type=F32).astype(BF) for ref in (own_ref, partner_ref)]
        taps.append(jnp.concatenate(pair, axis=0))
    for g in range(channels // CG):
        columns = slice(g * CG, (g + 1) * CG)
        total = jnp.zeros((2 * count, CG), F32)
        for t in range(RATE):
            weight = w_ref[t * CG : (t + 1) * CG, columns]
            total += jnp.dot(taps[t][:, columns], weight, preferred_element_type=F32)
        out_ref[:, columns] = total.astype(BF)


def compress(own, partner, conv_weight):
    count, channels = own.shape
    return pl.pallas_call(
        compress_kernel,
        out_shape=jax.ShapeDtypeStruct((2 * count // RATE, channels), BF),
        in_specs=[VMEM, VMEM, VMEM],
        out_specs=VMEM,
        cost_estimate=cost(5),
        name="compress",
    )(own, partner, conv_weight)


def weight_copies(buffer, sems, owns, nears, fars, far_order):
    plane, group = lax.axis_index("seq"), lax.axis_index("groups")
    depth = owns[0][0].shape[0]
    half = depth // 2
    pieces = [(ref.at[:, columns], aligned(plane, depth), place) for ref, columns, place in owns]
    for distance, near in enumerate(nears, 1):
        if near.shape[0] == depth:
            pieces.append((near, aligned(plane ^ distance, depth), slice(None)))
        else:
            pieces.append((near, aligned((plane ^ distance) * 2 + group, half), slice(None)))
    order = iter(far_order)
    for far in fars:
        for i in range(far.shape[0] // half):
            place = aligned((plane ^ next(order)) * 2 + 1 - group, half)
            pieces.append((far.at[pl.ds(i * half, half), :], place, slice(None)))
    copies = []
    for ref, rows, place in pieces:
        copies.append(pltpu.make_async_copy(ref, buffer.at[rows, place], sems.at[len(copies)]))
    return copies


def block_owner(index, tensor_size, sub_size):
    tensor, sub = lax.axis_index("tensor"), lax.axis_index("sub")
    return (tensor ^ (index // sub_size)) * sub_size + (sub ^ (index % sub_size))


def memory_kernel(planes, tensor_size, sub_size, far_order, halves, *refs):
    blocks = tensor_size * sub_size
    wk, wv = refs[:2]
    nears, fars, refs = refs[2 : planes + 1], refs[planes + 1 : planes + 1 + halves], refs[planes + 1 + halves :]
    pieces, (out, wbuf, xbuf, acc, xsem, wsem) = refs[:blocks], refs[blocks:]
    width = wbuf.shape[1] // 2
    columns = aligned(lax.axis_index("seq") & 1, width)
    owns = [(wk, columns, slice(0, width)), (wv, columns, slice(width, 2 * width))]
    wcopies = weight_copies(wbuf, wsem, owns, nears, fars, far_order)
    xcopies = [pltpu.make_async_copy(pieces[j], xbuf.at[j], xsem.at[j]) for j in range(blocks)]
    for copy in wcopies + xcopies:
        copy.start()
    for copy in wcopies:
        copy.wait()
    product_loop(tensor_size, sub_size, xbuf, wbuf, acc, out, xcopies)


def product_loop(tensor_size, sub_size, xbuf, wbuf, acc, out, waits=()):
    blocks, chunk = xbuf.shape[0], xbuf.shape[2]
    for j in range(blocks):
        if waits:
            waits[j].wait()
        weight = aligned(block_owner(j, tensor_size, sub_size), chunk)
        part = jnp.dot(xbuf[j], wbuf[weight, :], preferred_element_type=F32)
        if j:
            part += acc[...]
        if j < blocks - 1:
            acc[...] = part
        else:
            out[...] = part.astype(BF)


def project_memory(planes, tensor_size, sub_size, wk, wv, nears, fars, far_order, pieces):
    depth, columns = wk.shape
    blocks, (rows, chunk) = len(pieces), pieces[0].shape
    operands = [wk, wv, *nears, *fars, *pieces]
    return pl.pallas_call(
        functools.partial(memory_kernel, planes, tensor_size, sub_size, far_order, len(fars)),
        out_shape=[jax.ShapeDtypeStruct((rows, columns), BF), pltpu.VMEM((depth * planes, columns), BF)],
        in_specs=[ANY] * len(operands),
        out_specs=[VMEM, VMEM],
        scratch_shapes=[
            pltpu.VMEM((blocks, rows, chunk), BF),
            pltpu.VMEM((rows, columns), F32),
            pltpu.SemaphoreType.DMA((blocks,)),
            pltpu.SemaphoreType.DMA((2 + 2 * (planes - 1),)),
        ],
        compiler_params=pltpu.CompilerParams(vmem_limit_bytes=MEMORY_LIMIT),
        cost_estimate=cost(4),
        name="project_memory",
    )(*operands)


def tokens_kernel(tensor_size, sub_size, *refs):
    blocks = tensor_size * sub_size
    pieces, (wbuf, out, xbuf, acc, sems) = refs[: 2 * blocks], refs[2 * blocks :]
    rows, chunk = pieces[0].shape
    copies = []
    for j in range(blocks):
        for side in range(2):
            dest = xbuf.at[j, pl.ds(side * rows, rows), :]
            copies.append(pltpu.make_async_copy(pieces[side * blocks + j], dest, sems.at[len(copies)]))
    for copy in copies:
        copy.start()
    for j in range(blocks):
        weight = aligned(block_owner(j, tensor_size, sub_size), chunk)
        for side in range(2):
            copies[2 * j + side].wait()
            here = slice(side * rows, (side + 1) * rows)
            part = jnp.dot(xbuf[j, here, :], wbuf[weight, :], preferred_element_type=F32)
            if j:
                part += acc[here, :]
            if j < blocks - 1:
                acc[here, :] = part
            else:
                out[here, :] = part.astype(BF)


def project_tokens(tensor_size, sub_size, own, partner, weights):
    blocks, (rows, chunk), columns = len(own), own[0].shape, weights.shape[1]
    return pl.pallas_call(
        functools.partial(tokens_kernel, tensor_size, sub_size),
        out_shape=[pltpu.VMEM((2 * rows, columns), BF), pltpu.VMEM((blocks, 2 * rows, chunk), BF)],
        in_specs=[ANY] * (2 * blocks) + [VMEM],
        out_specs=[VMEM, VMEM],
        scratch_shapes=[pltpu.VMEM((2 * rows, columns), F32), pltpu.SemaphoreType.DMA((2 * blocks,))],
        compiler_params=pltpu.CompilerParams(vmem_limit_bytes=TOKENS_LIMIT),
        cost_estimate=cost(6),
        name="project_tokens",
    )(*own, *partner, resident(weights))


SCALE = HD ** (-0.5) * math.log2(math.e)
CONTRACT = (((1,), (1,)), ((), ()))


def local_kernel(side, planes, tensor_size, sub_size, far_order, halves, *refs):
    refs = refs[1:]
    if halves is None:
        wbuf, xbuf, kvbuf, queries, sums, largest, totals = refs
    else:
        wq, refs = refs[0], refs[1:]
        nears, fars, refs = refs[: planes - 1], refs[planes - 1 : planes - 1 + halves], refs[planes - 1 + halves :]
        xbuf, kvbuf, queries, sums, largest, totals, wbuf, wsem = refs
        owns = [(wq, aligned(lax.axis_index("seq") & 1, wbuf.shape[1]), slice(None))]
        run_copies(weight_copies(wbuf, wsem, owns, nears, fars, far_order))
    rows_here, width = queries.shape
    here = pl.ds(side * rows_here, rows_here)
    product_loop(tensor_size, sub_size, xbuf.at[:, here, :], wbuf, sums, queries)
    row = lax.broadcasted_iota(jnp.int32, (SEG, SEG), 0)
    causal = row >= lax.broadcasted_iota(jnp.int32, (SEG, SEG), 1)
    for a in range(rows_here // SEG):
        rows = slice(a * SEG, (a + 1) * SEG)
        kvrows = slice(side * rows_here + a * SEG, side * rows_here + (a + 1) * SEG)
        for h in range(width // HD):
            ks, vs = slice(h * HD, (h + 1) * HD), slice(width + h * HD, width + (h + 1) * HD)
            scores = lax.dot_general(queries[rows, ks], kvbuf[kvrows, ks], CONTRACT, preferred_element_type=F32)
            scores = jnp.where(causal, scores * SCALE, -jnp.inf)
            best = jnp.max(scores, axis=1, keepdims=True)
            weights = jnp.exp2(scores - best)
            largest[rows, ks] = jnp.broadcast_to(best, (SEG, HD))
            totals[rows, ks] = jnp.broadcast_to(jnp.sum(weights, axis=1, keepdims=True), (SEG, HD))
            sums[rows, ks] = jnp.dot(weights.astype(BF), kvbuf[kvrows, vs], preferred_element_type=F32)


def attend_local(side, planes, tensor_size, sub_size, turn, weight, far_order, held, kv_tok):
    rows, width = held.shape[1] // 2, kv_tok.shape[1] // 2
    state = [pltpu.VMEM((rows, width), BF)] + [pltpu.VMEM((rows, width), F32)] * 3
    scratch, halves = [], None
    if isinstance(weight, tuple):
        wq, nears, fars = weight
        operands, halves = [wq, *nears, *fars], len(fars)
        specs = [ANY] * len(operands)
        state.append(pltpu.VMEM((wq.shape[0] * planes, width), BF))
        scratch = [pltpu.SemaphoreType.DMA((planes + len(far_order),))]
    else:
        operands, specs = [resident(weight)], [VMEM]
    return pl.pallas_call(
        functools.partial(local_kernel, side, planes, tensor_size, sub_size, far_order, halves),
        out_shape=state,
        in_specs=[SMEM] + specs + [VMEM] * 2,
        out_specs=[VMEM] * len(state),
        scratch_shapes=scratch,
        compiler_params=pltpu.CompilerParams(vmem_limit_bytes=VMEM_LIMIT),
        cost_estimate=cost(4),
        name="attend_local",
    )(turn, *operands, resident(held), resident(kv_tok))


def far_kernel(side, planes, segments, length, queries, sums, largest, totals, *refs):
    mems, (out, membuf, obuf, sems) = refs[: planes // 2], refs[planes // 2 :]
    plane = lax.axis_index("seq")
    rows_here, width = obuf.shape
    slots = rows_here // SEG
    count = mems[0].shape[0]
    copies = []
    for i, mem in enumerate(mems):
        copies.append(pltpu.make_async_copy(mem, membuf.at[pl.ds(i * count, count), :], sems.at[1 + i]))
        copies[-1].start()
    per_plane = count // 2
    mem_total = membuf.shape[0]
    column = lax.broadcasted_iota(jnp.int32, (1, mem_total), 1)
    owner = jnp.zeros((1, mem_total), jnp.int32)
    for distance in range(planes):
        for i in range(slots):
            start = distance * per_plane + i * MEM
            inside = (column >= start) & (column < start + MEM)
            owner = jnp.where(inside, segments[(plane ^ distance) * slots + i], owner)
    position = lax.broadcasted_iota(jnp.int32, (SEG, HD), 0)
    for copy in copies:
        copy.wait()
    for a in range(slots):
        rows = slice(a * SEG, (a + 1) * SEG)
        segment = segments[(plane ^ side) * slots + a]
        allowed = owner < segment
        valid = position + segment * SEG < length[0]
        for h in range(width // HD):
            ks, vs = slice(h * HD, (h + 1) * HD), slice(width + h * HD, width + (h + 1) * HD)
            scores = lax.dot_general(queries[rows, ks], membuf[:, ks], CONTRACT, preferred_element_type=F32)
            scores = jnp.where(allowed, scores * SCALE, -jnp.inf)
            before = largest[rows, ks]
            best = jnp.maximum(before[:, :1], jnp.max(scores, axis=1, keepdims=True))
            weights = jnp.exp2(scores - best)
            factor = jnp.exp2(before - best)
            denominator = totals[rows, ks] * factor + jnp.sum(weights, axis=1, keepdims=True)
            numerator = sums[rows, ks] * factor
            numerator += jnp.dot(weights.astype(BF), membuf[:, vs], preferred_element_type=F32)
            obuf[rows, ks] = jnp.where(valid, numerator / denominator, 0.0).astype(BF)
    dest = out if side else out.at[:, aligned(plane & 1, width)]
    copy = pltpu.make_async_copy(obuf, dest, sems.at[0])
    copy.start()
    copy.wait()


def attend(side, planes, segments, length, state, mems):
    rows, width = state[0].shape
    mem_total = len(mems) * mems[0].shape[0]
    operands = [segments, length, *(resident(value) for value in state), *mems]
    return pl.pallas_call(
        functools.partial(far_kernel, side, planes),
        out_shape=jax.ShapeDtypeStruct((rows, width if side else 2 * width), BF),
        in_specs=[SMEM, SMEM] + [VMEM] * len(state) + [ANY] * len(mems),
        out_specs=ANY,
        scratch_shapes=[
            pltpu.VMEM((mem_total, 2 * width), BF),
            pltpu.VMEM((rows, width), BF),
            pltpu.SemaphoreType.DMA((1 + len(mems),)),
        ],
        compiler_params=pltpu.CompilerParams(vmem_limit_bytes=VMEM_LIMIT),
        cost_estimate=cost(4),
        name="attend",
    )(*operands)


def on_device(
    activations, conv_weight, query_weight, key_weight, value_weight, segment_for_slot, book_length
):
    planes, tensor_size, sub_size = (lax.axis_size(name) for name in ("seq", "tensor", "sub"))
    parity = lax.axis_index("seq") & 1

    kv_same, kv_other, q_same, q_other, q_whole = split_weights(key_weight, value_weight, query_weight)

    def across(block, label):
        return {f"{label}x{k}": (block, "tensor", k) for k in range(1, tensor_size)}

    def within(block, label):
        return {f"{label}c{k}": (block, "sub", k) for k in range(1, sub_size)}

    def distant(distances, name):
        same, other = {"kv": (kv_same, kv_other), "q": (q_same, q_other)}[name]
        return {f"{name}{d}": (other if d & 1 else same, "seq", d) for d in distances}

    def relayed(distances, name):
        return {f"y{name}{d}": (got[f"{name}{d}"], "groups", 1) for d in distances}

    got = {}

    def stage(sends, *computed):
        held = tuple(got[key] for key in fresh)
        new = {}
        for key, (value, axis, distance) in sends.items():
            new[key] = swap(after(value, *held), axis, distance, key)
        ended = lax.optimization_barrier(tuple(new.values()) + computed)
        got.update(zip(new, ended))
        fresh[:] = list(new)
        return ended[len(new) :]

    fresh = []
    every = range(1, planes)
    first = [2] if planes > 2 else []
    second = [d for d in every[::-1] if d not in first]
    stage(
        {"Xz": (activations, "seq", 1)}
        | across(activations, "A")
        | within(activations, "A0")
        | distant(first, "kv")
    )
    partner = got["Xz"]
    sends = across(partner, "B") | distant(second, "kv") | relayed(first, "kv")
    (both,) = stage(sends, compress(activations, partner, conv_weight))
    far_planes = range(2, planes)
    second_kv = jnp.concatenate([got[f"kv{d}"] for d in second], axis=0)
    stage(
        distant(far_planes, "q")
        | {"q1": (q_whole, "seq", 1), "ykv": (second_kv, "groups", 1)}
        | across(both, "C")
    )
    sends = within(both, "C0") | within(partner, "B0") | relayed(far_planes, "q")
    for label in ("C", "B", "A"):
        for k in range(1, tensor_size):
            sends |= within(got[f"{label}x{k}"], f"{label}{k}")
    before = tuple(got[key] for key in fresh)
    for key, (value, axis, distance) in sends.items():
        held = before if axis == "groups" else ()
        got[key] = swap(after(value, *held), axis, distance, key)

    def pieces(block, label):
        whole = []
        for k in range(tensor_size):
            whole.append(got[f"{label}x{k}"] if k else block)
            whole += [got[f"{label}{k}c{u}"] for u in range(1, sub_size)]
        return whole

    own_pieces, partner_pieces = pieces(activations, "A"), pieces(partner, "B")
    compressed_pieces = pieces(both, "C")
    sizes = (planes, tensor_size, sub_size)
    kv_parts = ([got[f"kv{d}"] for d in every], [got[f"ykv{d}"] for d in first] + [got["ykv"]], first + second)
    kv_mem, kv_held = project_memory(*sizes, key_weight, value_weight, *kv_parts, compressed_pieces)
    mems = [kv_mem] + [swap(kv_mem, "seq", d, f"m{d}") for d in range(2, planes, 2)]
    kv_tok, held = project_tokens(tensor_size, sub_size, own_pieces, partner_pieces, kv_held)
    q_parts = (query_weight, [got[f"q{d}"] for d in every], [got[f"yq{d}"] for d in far_planes])
    q_order = list(far_planes)
    *state, q_held = attend_local(1, *sizes, segment_for_slot, q_parts, q_order, held, kv_tok)
    theirs = attend(1, planes, segment_for_slot, book_length, state, mems)
    returned = swap(theirs, "seq", 1, "ctx")
    turn = after(segment_for_slot, theirs)
    state = attend_local(0, *sizes, turn, q_held, q_order, held, kv_tok)
    mine = attend(0, planes, segment_for_slot, book_length, state, mems)
    return lax.dynamic_update_slice(mine, returned, (0, (1 - parity) * theirs.shape[1]))


def solution(mesh):
    placed = (
        P(("groups", "seq"), ("tensor", "sub")),
        P(None, ("tensor", "sub")),
        P("seq", ("tensor", "sub")),
        P("seq", ("tensor", "sub")),
        P("seq", ("tensor", "sub")),
        P("groups"),
        P("groups"),
    )
    return jax.shard_map(
        on_device,
        mesh=mesh,
        in_specs=placed,
        out_specs=P(("groups", "seq"), ("tensor", "sub")),
        check_vma=False,
    )
```

```python
import functools
import math

import jax
import jax.numpy as jnp
from jax import lax
from jax.experimental import pallas as pl
from jax.experimental.pallas import tpu as pltpu
from jax.sharding import PartitionSpec as P

HD = 128
CG = 128
RATE = 4
SEG = 256
MEM = 64
BF = jnp.bfloat16


def cost(microseconds):
    return pl.CostEstimate(flops=int(microseconds * 1.0e9), bytes_accessed=1000, transcendentals=0)
F32 = jnp.float32
ANY = pl.BlockSpec(memory_space=pl.ANY)
MEMORY_LIMIT, TOKENS_LIMIT, VMEM_LIMIT = 48 << 20, 38 << 20, 26 << 20
SMEM = pl.BlockSpec(memory_space=pltpu.SMEM)
VMEM = pl.BlockSpec(memory_space=pltpu.VMEM)


EARLY = 2


def swap(value, axis, distance, label):
    size = lax.axis_size(axis)
    with jax.named_scope("L_" + label):
        return lax.ppermute(value, axis, [(i, i ^ distance) for i in range(size)])


def after(value, *others):
    return lax.optimization_barrier((value,) + others)[0]


def resident(value):
    return pltpu.with_memory_space_constraint(value, pltpu.VMEM)


def run_copies(copies):
    for copy in copies:
        copy.start()
    for copy in copies:
        copy.wait()


def aligned(index, size):
    return pl.ds(pl.multiple_of(index * size, size), size)


def split_kernel(wk, wv, wq, kv_same, kv_other, q_same, q_other, q_whole, sems):
    group, parity = lax.axis_index("groups"), lax.axis_index("seq") & 1
    half, width = q_same.shape
    rows = aligned(group, half)
    copies = []
    for target, kv, q in ((parity, kv_same, q_same), (1 - parity, kv_other, q_other)):
        columns = aligned(target, width)
        for source, dest in ((wk, kv.at[:, 0:width]), (wv, kv.at[:, width : 2 * width]), (wq, q)):
            copies.append(pltpu.make_async_copy(source.at[rows, columns], dest, sems.at[len(copies)]))
    source = wq.at[:, aligned(1 - parity, width)]
    copies.append(pltpu.make_async_copy(source, q_whole, sems.at[len(copies)]))
    run_copies(copies)


def split_weights(wk, wv, wq):
    depth, columns = wk.shape
    half, width = depth // 2, columns // 2
    shapes = [(half, 2 * width), (half, 2 * width), (half, width), (half, width), (depth, width)]
    return pl.pallas_call(
        split_kernel,
        out_shape=[jax.ShapeDtypeStruct(s, BF) for s in shapes],
        in_specs=[ANY] * 3,
        out_specs=[VMEM] * 5,
        scratch_shapes=[pltpu.SemaphoreType.DMA((7,))],
        cost_estimate=cost(2),
        name="split_weights",
    )(wk, wv, wq)


def compress_kernel(own_ref, partner_ref, w_ref, out_ref):
    rows, channels = own_ref.shape
    count = rows // RATE
    row = lax.broadcasted_iota(jnp.int32, (count, rows), 0)
    column = lax.broadcasted_iota(jnp.int32, (count, rows), 1)
    taps = []
    for t in range(RATE):
        pick = (column == row * RATE + t).astype(BF)
        pair = [jnp.dot(pick, ref[...], preferred_element_type=F32).astype(BF) for ref in (own_ref, partner_ref)]
        taps.append(jnp.concatenate(pair, axis=0))
    for g in range(channels // CG):
        columns = slice(g * CG, (g + 1) * CG)
        total = jnp.zeros((2 * count, CG), F32)
        for t in range(RATE):
            weight = w_ref[t * CG : (t + 1) * CG, columns]
            total += jnp.dot(taps[t][:, columns], weight, preferred_element_type=F32)
        out_ref[:, columns] = total.astype(BF)


def compress(own, partner, conv_weight):
    count, channels = own.shape
    return pl.pallas_call(
        compress_kernel,
        out_shape=jax.ShapeDtypeStruct((2 * count // RATE, channels), BF),
        in_specs=[VMEM, VMEM, VMEM],
        out_specs=VMEM,
        cost_estimate=cost(5),
        name="compress",
    )(own, partner, conv_weight)


def weight_copies(buffer, sems, owns, nears, fars, far_order):
    plane, group = lax.axis_index("seq"), lax.axis_index("groups")
    depth = owns[0][0].shape[0]
    half = depth // 2
    pieces = [(ref.at[:, columns], aligned(plane, depth), place) for ref, columns, place in owns]
    for distance, near in enumerate(nears, 1):
        if near.shape[0] == depth:
            pieces.append((near, aligned(plane ^ distance, depth), slice(None)))
        else:
            pieces.append((near, aligned((plane ^ distance) * 2 + group, half), slice(None)))
    order = iter(far_order)
    for far in fars:
        for i in range(far.shape[0] // half):
            place = aligned((plane ^ next(order)) * 2 + 1 - group, half)
            pieces.append((far.at[pl.ds(i * half, half), :], place, slice(None)))
    copies = []
    for ref, rows, place in pieces:
        copies.append(pltpu.make_async_copy(ref, buffer.at[rows, place], sems.at[len(copies)]))
    return copies


def block_owner(index, tensor_size, sub_size):
    tensor, sub = lax.axis_index("tensor"), lax.axis_index("sub")
    return (tensor ^ (index // sub_size)) * sub_size + (sub ^ (index % sub_size))


def memory_kernel(planes, tensor_size, sub_size, far_order, halves, *refs):
    blocks = tensor_size * sub_size
    wk, wv = refs[:2]
    nears, fars, refs = refs[2 : planes + 1], refs[planes + 1 : planes + 1 + halves], refs[planes + 1 + halves :]
    pieces, (out, wbuf, xbuf, acc, xsem, wsem) = refs[:blocks], refs[blocks:]
    width = wbuf.shape[1] // 2
    columns = aligned(lax.axis_index("seq") & 1, width)
    owns = [(wk, columns, slice(0, width)), (wv, columns, slice(width, 2 * width))]
    wcopies = weight_copies(wbuf, wsem, owns, nears, fars, far_order)
    xcopies = [pltpu.make_async_copy(pieces[j], xbuf.at[j], xsem.at[j]) for j in range(blocks)]
    for copy in wcopies + xcopies:
        copy.start()
    for copy in wcopies:
        copy.wait()
    product_loop(tensor_size, sub_size, xbuf, wbuf, acc, out, xcopies)


def product_loop(tensor_size, sub_size, xbuf, wbuf, acc, out, waits=()):
    blocks, chunk = xbuf.shape[0], xbuf.shape[2]
    for j in range(blocks):
        if waits:
            waits[j].wait()
        weight = aligned(block_owner(j, tensor_size, sub_size), chunk)
        part = jnp.dot(xbuf[j], wbuf[weight, :], preferred_element_type=F32)
        if j:
            part += acc[...]
        if j < blocks - 1:
            acc[...] = part
        else:
            out[...] = part.astype(BF)


def project_memory(planes, tensor_size, sub_size, wk, wv, nears, fars, far_order, pieces):
    depth, columns = wk.shape
    blocks, (rows, chunk) = len(pieces), pieces[0].shape
    operands = [wk, wv, *nears, *fars, *pieces]
    return pl.pallas_call(
        functools.partial(memory_kernel, planes, tensor_size, sub_size, far_order, len(fars)),
        out_shape=[jax.ShapeDtypeStruct((rows, columns), BF), pltpu.VMEM((depth * planes, columns), BF)],
        in_specs=[ANY] * len(operands),
        out_specs=[VMEM, VMEM],
        scratch_shapes=[
            pltpu.VMEM((blocks, rows, chunk), BF),
            pltpu.VMEM((rows, columns), F32),
            pltpu.SemaphoreType.DMA((blocks,)),
            pltpu.SemaphoreType.DMA((2 + 2 * (planes - 1),)),
        ],
        compiler_params=pltpu.CompilerParams(vmem_limit_bytes=MEMORY_LIMIT),
        cost_estimate=cost(4),
        name="project_memory",
    )(*operands)


def tokens_kernel(tensor_size, sub_size, *refs):
    blocks = tensor_size * sub_size
    pieces, (wbuf, out, xbuf, acc, sems) = refs[: 2 * blocks], refs[2 * blocks :]
    rows, chunk = pieces[0].shape
    copies = []
    for j in range(blocks):
        for side in range(2):
            dest = xbuf.at[j, pl.ds(side * rows, rows), :]
            copies.append(pltpu.make_async_copy(pieces[side * blocks + j], dest, sems.at[len(copies)]))
    for copy in copies:
        copy.start()
    for j in range(blocks):
        weight = aligned(block_owner(j, tensor_size, sub_size), chunk)
        for side in range(2):
            copies[2 * j + side].wait()
            here = slice(side * rows, (side + 1) * rows)
            part = jnp.dot(xbuf[j, here, :], wbuf[weight, :], preferred_element_type=F32)
            if j:
                part += acc[here, :]
            if j < blocks - 1:
                acc[here, :] = part
            else:
                out[here, :] = part.astype(BF)


def project_tokens(tensor_size, sub_size, own, partner, weights):
    blocks, (rows, chunk), columns = len(own), own[0].shape, weights.shape[1]
    return pl.pallas_call(
        functools.partial(tokens_kernel, tensor_size, sub_size),
        out_shape=[pltpu.VMEM((2 * rows, columns), BF), pltpu.VMEM((blocks, 2 * rows, chunk), BF)],
        in_specs=[ANY] * (2 * blocks) + [VMEM],
        out_specs=[VMEM, VMEM],
        scratch_shapes=[pltpu.VMEM((2 * rows, columns), F32), pltpu.SemaphoreType.DMA((2 * blocks,))],
        compiler_params=pltpu.CompilerParams(vmem_limit_bytes=TOKENS_LIMIT),
        cost_estimate=cost(6),
        name="project_tokens",
    )(*own, *partner, resident(weights))


SCALE = HD ** (-0.5) * math.log2(math.e)
CONTRACT = (((1,), (1,)), ((), ()))


def local_kernel(side, planes, tensor_size, sub_size, far_order, halves, *refs):
    refs = refs[1:]
    if halves is None:
        wbuf, xbuf, kvbuf, queries, sums, largest, totals = refs
    else:
        wq, refs = refs[0], refs[1:]
        nears, fars, refs = refs[: planes - 1], refs[planes - 1 : planes - 1 + halves], refs[planes - 1 + halves :]
        xbuf, kvbuf, queries, sums, largest, totals, wbuf, wsem = refs
        owns = [(wq, aligned(lax.axis_index("seq") & 1, wbuf.shape[1]), slice(None))]
        run_copies(weight_copies(wbuf, wsem, owns, nears, fars, far_order))
    rows_here, width = queries.shape
    here = pl.ds(side * rows_here, rows_here)
    product_loop(tensor_size, sub_size, xbuf.at[:, here, :], wbuf, sums, queries)
    row = lax.broadcasted_iota(jnp.int32, (SEG, SEG), 0)
    causal = row >= lax.broadcasted_iota(jnp.int32, (SEG, SEG), 1)
    for a in range(rows_here // SEG):
        rows = slice(a * SEG, (a + 1) * SEG)
        kvrows = slice(side * rows_here + a * SEG, side * rows_here + (a + 1) * SEG)
        for h in range(width // HD):
            ks, vs = slice(h * HD, (h + 1) * HD), slice(width + h * HD, width + (h + 1) * HD)
            scores = lax.dot_general(queries[rows, ks], kvbuf[kvrows, ks], CONTRACT, preferred_element_type=F32)
            scores = jnp.where(causal, scores * SCALE, -jnp.inf)
            best = jnp.max(scores, axis=1, keepdims=True)
            weights = jnp.exp2(scores - best)
            largest[rows, ks] = jnp.broadcast_to(best, (SEG, HD))
            totals[rows, ks] = jnp.broadcast_to(jnp.sum(weights, axis=1, keepdims=True), (SEG, HD))
            sums[rows, ks] = jnp.dot(weights.astype(BF), kvbuf[kvrows, vs], preferred_element_type=F32)


def attend_local(side, planes, tensor_size, sub_size, turn, weight, far_order, held, kv_tok):
    rows, width = held.shape[1] // 2, kv_tok.shape[1] // 2
    state = [pltpu.VMEM((rows, width), BF)] + [pltpu.VMEM((rows, width), F32)] * 3
    scratch, halves = [], None
    if isinstance(weight, tuple):
        wq, nears, fars = weight
        operands, halves = [wq, *nears, *fars], len(fars)
        specs = [ANY] * len(operands)
        state.append(pltpu.VMEM((wq.shape[0] * planes, width), BF))
        scratch = [pltpu.SemaphoreType.DMA((planes + len(far_order),))]
    else:
        operands, specs = [resident(weight)], [VMEM]
    return pl.pallas_call(
        functools.partial(local_kernel, side, planes, tensor_size, sub_size, far_order, halves),
        out_shape=state,
        in_specs=[SMEM] + specs + [VMEM] * 2,
        out_specs=[VMEM] * len(state),
        scratch_shapes=scratch,
        compiler_params=pltpu.CompilerParams(vmem_limit_bytes=VMEM_LIMIT),
        cost_estimate=cost(4),
        name="attend_local",
    )(turn, *operands, resident(held), resident(kv_tok))


def far_kernel(side, planes, segments, length, queries, sums, largest, totals, *refs):
    mems, (out, membuf, obuf, sems) = refs[: planes // 2], refs[planes // 2 :]
    plane = lax.axis_index("seq")
    rows_here, width = obuf.shape
    slots = rows_here // SEG
    count = mems[0].shape[0]
    copies = []
    for i, mem in enumerate(mems):
        copies.append(pltpu.make_async_copy(mem, membuf.at[pl.ds(i * count, count), :], sems.at[1 + i]))
        copies[-1].start()
    per_plane = count // 2
    mem_total = membuf.shape[0]
    column = lax.broadcasted_iota(jnp.int32, (1, mem_total), 1)
    owner = jnp.zeros((1, mem_total), jnp.int32)
    for distance in range(planes):
        for i in range(slots):
            start = distance * per_plane + i * MEM
            inside = (column >= start) & (column < start + MEM)
            owner = jnp.where(inside, segments[(plane ^ distance) * slots + i], owner)
    position = lax.broadcasted_iota(jnp.int32, (SEG, HD), 0)
    for copy in copies:
        copy.wait()
    for a in range(slots):
        rows = slice(a * SEG, (a + 1) * SEG)
        segment = segments[(plane ^ side) * slots + a]
        allowed = owner < segment
        valid = position + segment * SEG < length[0]
        for h in range(width // HD):
            ks, vs = slice(h * HD, (h + 1) * HD), slice(width + h * HD, width + (h + 1) * HD)
            scores = lax.dot_general(queries[rows, ks], membuf[:, ks], CONTRACT, preferred_element_type=F32)
            scores = jnp.where(allowed, scores * SCALE, -jnp.inf)
            before = largest[rows, ks]
            best = jnp.maximum(before[:, :1], jnp.max(scores, axis=1, keepdims=True))
            weights = jnp.exp2(scores - best)
            factor = jnp.exp2(before - best)
            denominator = totals[rows, ks] * factor + jnp.sum(weights, axis=1, keepdims=True)
            numerator = sums[rows, ks] * factor
            numerator += jnp.dot(weights.astype(BF), membuf[:, vs], preferred_element_type=F32)
            obuf[rows, ks] = jnp.where(valid, numerator / denominator, 0.0).astype(BF)
    dest = out if side else out.at[:, aligned(plane & 1, width)]
    copy = pltpu.make_async_copy(obuf, dest, sems.at[0])
    copy.start()
    copy.wait()


def attend(side, planes, segments, length, state, mems):
    rows, width = state[0].shape
    mem_total = len(mems) * mems[0].shape[0]
    operands = [segments, length, *(resident(value) for value in state), *mems]
    return pl.pallas_call(
        functools.partial(far_kernel, side, planes),
        out_shape=jax.ShapeDtypeStruct((rows, width if side else 2 * width), BF),
        in_specs=[SMEM, SMEM] + [VMEM] * len(state) + [ANY] * len(mems),
        out_specs=ANY,
        scratch_shapes=[
            pltpu.VMEM((mem_total, 2 * width), BF),
            pltpu.VMEM((rows, width), BF),
            pltpu.SemaphoreType.DMA((1 + len(mems),)),
        ],
        compiler_params=pltpu.CompilerParams(vmem_limit_bytes=VMEM_LIMIT),
        cost_estimate=cost(4),
        name="attend",
    )(*operands)


def on_device(
    activations, conv_weight, query_weight, key_weight, value_weight, segment_for_slot, book_length
):
    planes, tensor_size, sub_size = (lax.axis_size(name) for name in ("seq", "tensor", "sub"))
    parity = lax.axis_index("seq") & 1

    kv_same, kv_other, q_same, q_other, q_whole = split_weights(key_weight, value_weight, query_weight)

    def across(block, label):
        return {f"{label}x{k}": (block, "tensor", k) for k in range(1, tensor_size)}

    def within(block, label):
        return {f"{label}c{k}": (block, "sub", k) for k in range(1, sub_size)}

    def distant(distances, name):
        same, other = {"kv": (kv_same, kv_other), "q": (q_same, q_other)}[name]
        return {f"{name}{d}": (other if d & 1 else same, "seq", d) for d in distances}

    def relayed(distances, name):
        return {f"y{name}{d}": (got[f"{name}{d}"], "groups", 1) for d in distances}

    got = {}

    def stage(sends, *computed):
        held = tuple(got[key] for key in fresh)
        new = {}
        for key, (value, axis, distance) in sends.items():
            new[key] = swap(after(value, *held), axis, distance, key)
        ended = lax.optimization_barrier(tuple(new.values()) + computed)
        got.update(zip(new, ended))
        fresh[:] = list(new)
        return ended[len(new) :]

    fresh = []
    every = range(1, planes)
    first = [2] if planes > 2 else []
    second = [d for d in every[::-1] if d not in first]
    stage(
        {"Xz": (activations, "seq", 1)}
        | across(activations, "A")
        | within(activations, "A0")
        | distant(first, "kv")
    )
    partner = got["Xz"]
    sends = across(partner, "B") | distant(second, "kv") | relayed(first, "kv")
    both = compress(activations, partner, conv_weight)
    hops = {f"C0c{k}": swap(both, "sub", k, f"C0c{k}") for k in range(1, sub_size)}
    both, *ended = stage(sends, both, *hops.values())
    got.update(zip(hops, ended))
    far_planes = range(2, planes)
    second_kv = jnp.concatenate([got[f"kv{d}"] for d in second], axis=0)
    stage(
        distant(far_planes, "q")
        | {"q1": (q_whole, "seq", 1), "ykv": (second_kv, "groups", 1)}
        | across(both, "C")
    )
    sends = within(partner, "B0") | relayed(far_planes, "q")
    for label in ("C", "B", "A"):
        for k in range(1, tensor_size):
            sends |= within(got[f"{label}x{k}"], f"{label}{k}")
    before = tuple(got[key] for key in fresh)
    for key, (value, axis, distance) in sends.items():
        held = before if axis == "groups" else ()
        got[key] = swap(after(value, *held), axis, distance, key)

    def pieces(block, label):
        whole = []
        for k in range(tensor_size):
            whole.append(got[f"{label}x{k}"] if k else block)
            whole += [got[f"{label}{k}c{u}"] for u in range(1, sub_size)]
        return whole

    own_pieces, partner_pieces = pieces(activations, "A"), pieces(partner, "B")
    compressed_pieces = pieces(both, "C")
    sizes = (planes, tensor_size, sub_size)
    kv_parts = ([got[f"kv{d}"] for d in every], [got[f"ykv{d}"] for d in first] + [got["ykv"]], first + second)
    kv_mem, kv_held = project_memory(*sizes, key_weight, value_weight, *kv_parts, compressed_pieces)
    mems = [kv_mem] + [swap(kv_mem, "seq", d, f"m{d}") for d in range(2, planes, 2)]
    kv_tok, held = project_tokens(tensor_size, sub_size, own_pieces, partner_pieces, kv_held)
    q_parts = (query_weight, [got[f"q{d}"] for d in every], [got[f"yq{d}"] for d in far_planes])
    q_order = list(far_planes)
    *state, q_held = attend_local(1, *sizes, segment_for_slot, q_parts, q_order, held, kv_tok)
    theirs = attend(1, planes, segment_for_slot, book_length, state, mems)
    returned = swap(theirs, "seq", 1, "ctx")
    turn = after(segment_for_slot, theirs)
    state = attend_local(0, *sizes, turn, q_held, q_order, held, kv_tok)
    mine = attend(0, planes, segment_for_slot, book_length, state, mems)
    return lax.dynamic_update_slice(mine, returned, (0, (1 - parity) * theirs.shape[1]))


def solution(mesh):
    placed = (
        P(("groups", "seq"), ("tensor", "sub")),
        P(None, ("tensor", "sub")),
        P("seq", ("tensor", "sub")),
        P("seq", ("tensor", "sub")),
        P("seq", ("tensor", "sub")),
        P("groups"),
        P("groups"),
    )
    return jax.shard_map(
        on_device,
        mesh=mesh,
        in_specs=placed,
        out_specs=P(("groups", "seq"), ("tensor", "sub")),
        check_vma=False,
    )
```

```python
import functools
import math

import jax
import jax.numpy as jnp
from jax import lax
from jax.experimental import pallas as pl
from jax.experimental.pallas import tpu as pltpu
from jax.sharding import PartitionSpec as P

HD = 128
CG = 128
RATE = 4
SEG = 256
MEM = 64
BF = jnp.bfloat16


def cost(microseconds):
    return pl.CostEstimate(flops=int(microseconds * 1.0e9), bytes_accessed=1000, transcendentals=0)
F32 = jnp.float32
ANY = pl.BlockSpec(memory_space=pl.ANY)
MEMORY_LIMIT, TOKENS_LIMIT, VMEM_LIMIT = 48 << 20, 38 << 20, 26 << 20
SMEM = pl.BlockSpec(memory_space=pltpu.SMEM)
VMEM = pl.BlockSpec(memory_space=pltpu.VMEM)


EARLY = 2


def swap(value, axis, distance, label):
    size = lax.axis_size(axis)
    with jax.named_scope("L_" + label):
        return lax.ppermute(value, axis, [(i, i ^ distance) for i in range(size)])


def after(value, *others):
    return lax.optimization_barrier((value,) + others)[0]


def resident(value):
    return pltpu.with_memory_space_constraint(value, pltpu.VMEM)


def run_copies(copies):
    for copy in copies:
        copy.start()
    for copy in copies:
        copy.wait()


def aligned(index, size):
    return pl.ds(pl.multiple_of(index * size, size), size)


def split_kernel(wk, wv, wq, kv_same, kv_other, q_same, q_other, q_whole, sems):
    group, parity = lax.axis_index("groups"), lax.axis_index("seq") & 1
    half, width = q_same.shape
    rows = aligned(group, half)
    copies = []
    for target, kv, q in ((parity, kv_same, q_same), (1 - parity, kv_other, q_other)):
        columns = aligned(target, width)
        for source, dest in ((wk, kv.at[:, 0:width]), (wv, kv.at[:, width : 2 * width]), (wq, q)):
            copies.append(pltpu.make_async_copy(source.at[rows, columns], dest, sems.at[len(copies)]))
    source = wq.at[:, aligned(1 - parity, width)]
    copies.append(pltpu.make_async_copy(source, q_whole, sems.at[len(copies)]))
    run_copies(copies)


def split_weights(wk, wv, wq):
    depth, columns = wk.shape
    half, width = depth // 2, columns // 2
    shapes = [(half, 2 * width), (half, 2 * width), (half, width), (half, width), (depth, width)]
    return pl.pallas_call(
        split_kernel,
        out_shape=[jax.ShapeDtypeStruct(s, BF) for s in shapes],
        in_specs=[ANY] * 3,
        out_specs=[VMEM] * 5,
        scratch_shapes=[pltpu.SemaphoreType.DMA((7,))],
        cost_estimate=cost(2),
        name="split_weights",
    )(wk, wv, wq)


def compress_kernel(own_ref, partner_ref, w_ref, out_ref):
    rows, channels = own_ref.shape
    count = rows // RATE
    row = lax.broadcasted_iota(jnp.int32, (count, rows), 0)
    column = lax.broadcasted_iota(jnp.int32, (count, rows), 1)
    taps = []
    for t in range(RATE):
        pick = (column == row * RATE + t).astype(BF)
        pair = [jnp.dot(pick, ref[...], preferred_element_type=F32).astype(BF) for ref in (own_ref, partner_ref)]
        taps.append(jnp.concatenate(pair, axis=0))
    for g in range(channels // CG):
        columns = slice(g * CG, (g + 1) * CG)
        total = jnp.zeros((2 * count, CG), F32)
        for t in range(RATE):
            weight = w_ref[t * CG : (t + 1) * CG, columns]
            total += jnp.dot(taps[t][:, columns], weight, preferred_element_type=F32)
        out_ref[:, columns] = total.astype(BF)


def compress(own, partner, conv_weight):
    count, channels = own.shape
    return pl.pallas_call(
        compress_kernel,
        out_shape=jax.ShapeDtypeStruct((2 * count // RATE, channels), BF),
        in_specs=[VMEM, VMEM, VMEM],
        out_specs=VMEM,
        cost_estimate=cost(5),
        name="compress",
    )(own, partner, conv_weight)


def weight_copies(buffer, sems, owns, nears, fars, far_order):
    plane, group = lax.axis_index("seq"), lax.axis_index("groups")
    depth = owns[0][0].shape[0]
    half = depth // 2
    pieces = [(ref.at[:, columns], aligned(plane, depth), place) for ref, columns, place in owns]
    for distance, near in enumerate(nears, 1):
        if near.shape[0] == depth:
            pieces.append((near, aligned(plane ^ distance, depth), slice(None)))
        else:
            pieces.append((near, aligned((plane ^ distance) * 2 + group, half), slice(None)))
    order = iter(far_order)
    for far in fars:
        for i in range(far.shape[0] // half):
            place = aligned((plane ^ next(order)) * 2 + 1 - group, half)
            pieces.append((far.at[pl.ds(i * half, half), :], place, slice(None)))
    copies = []
    for ref, rows, place in pieces:
        copies.append(pltpu.make_async_copy(ref, buffer.at[rows, place], sems.at[len(copies)]))
    return copies


def block_owner(index, tensor_size, sub_size):
    tensor, sub = lax.axis_index("tensor"), lax.axis_index("sub")
    return (tensor ^ (index // sub_size)) * sub_size + (sub ^ (index % sub_size))


def memory_kernel(planes, tensor_size, sub_size, far_order, halves, *refs):
    blocks = tensor_size * sub_size
    wk, wv = refs[:2]
    nears, fars, refs = refs[2 : planes + 1], refs[planes + 1 : planes + 1 + halves], refs[planes + 1 + halves :]
    pieces, (out, wbuf, xbuf, acc, xsem, wsem) = refs[:blocks], refs[blocks:]
    width = wbuf.shape[1] // 2
    columns = aligned(lax.axis_index("seq") & 1, width)
    owns = [(wk, columns, slice(0, width)), (wv, columns, slice(width, 2 * width))]
    wcopies = weight_copies(wbuf, wsem, owns, nears, fars, far_order)
    xcopies = [pltpu.make_async_copy(pieces[j], xbuf.at[j], xsem.at[j]) for j in range(blocks)]
    for copy in wcopies + xcopies:
        copy.start()
    for copy in wcopies:
        copy.wait()
    product_loop(tensor_size, sub_size, xbuf, wbuf, acc, out, xcopies)


def product_loop(tensor_size, sub_size, xbuf, wbuf, acc, out, waits=()):
    blocks, chunk = xbuf.shape[0], xbuf.shape[2]
    for j in range(blocks):
        if waits:
            waits[j].wait()
        weight = aligned(block_owner(j, tensor_size, sub_size), chunk)
        part = jnp.dot(xbuf[j], wbuf[weight, :], preferred_element_type=F32)
        if j:
            part += acc[...]
        if j < blocks - 1:
            acc[...] = part
        else:
            out[...] = part.astype(BF)


def project_memory(planes, tensor_size, sub_size, wk, wv, nears, fars, far_order, pieces):
    depth, columns = wk.shape
    blocks, (rows, chunk) = len(pieces), pieces[0].shape
    operands = [wk, wv, *nears, *fars, *pieces]
    return pl.pallas_call(
        functools.partial(memory_kernel, planes, tensor_size, sub_size, far_order, len(fars)),
        out_shape=[jax.ShapeDtypeStruct((rows, columns), BF), pltpu.VMEM((depth * planes, columns), BF)],
        in_specs=[ANY] * len(operands),
        out_specs=[VMEM, VMEM],
        scratch_shapes=[
            pltpu.VMEM((blocks, rows, chunk), BF),
            pltpu.VMEM((rows, columns), F32),
            pltpu.SemaphoreType.DMA((blocks,)),
            pltpu.SemaphoreType.DMA((2 + 2 * (planes - 1),)),
        ],
        compiler_params=pltpu.CompilerParams(vmem_limit_bytes=MEMORY_LIMIT),
        cost_estimate=cost(4),
        name="project_memory",
    )(*operands)


def tokens_kernel(tensor_size, sub_size, *refs):
    blocks = tensor_size * sub_size
    pieces, (wbuf, out, xbuf, acc, sems) = refs[: 2 * blocks], refs[2 * blocks :]
    rows, chunk = pieces[0].shape
    copies = []
    for j in range(blocks):
        for side in range(2):
            dest = xbuf.at[j, pl.ds(side * rows, rows), :]
            copies.append(pltpu.make_async_copy(pieces[side * blocks + j], dest, sems.at[len(copies)]))
    for copy in copies:
        copy.start()
    for j in range(blocks):
        weight = aligned(block_owner(j, tensor_size, sub_size), chunk)
        for side in range(2):
            copies[2 * j + side].wait()
            here = slice(side * rows, (side + 1) * rows)
            part = jnp.dot(xbuf[j, here, :], wbuf[weight, :], preferred_element_type=F32)
            if j:
                part += acc[here, :]
            if j < blocks - 1:
                acc[here, :] = part
            else:
                out[here, :] = part.astype(BF)


def project_tokens(tensor_size, sub_size, own, partner, weights):
    blocks, (rows, chunk), columns = len(own), own[0].shape, weights.shape[1]
    return pl.pallas_call(
        functools.partial(tokens_kernel, tensor_size, sub_size),
        out_shape=[pltpu.VMEM((2 * rows, columns), BF), pltpu.VMEM((blocks, 2 * rows, chunk), BF)],
        in_specs=[ANY] * (2 * blocks) + [VMEM],
        out_specs=[VMEM, VMEM],
        scratch_shapes=[pltpu.VMEM((2 * rows, columns), F32), pltpu.SemaphoreType.DMA((2 * blocks,))],
        compiler_params=pltpu.CompilerParams(vmem_limit_bytes=TOKENS_LIMIT),
        cost_estimate=cost(6),
        name="project_tokens",
    )(*own, *partner, resident(weights))


SCALE = HD ** (-0.5) * math.log2(math.e)
CONTRACT = (((1,), (1,)), ((), ()))


def local_kernel(side, planes, tensor_size, sub_size, far_order, halves, *refs):
    refs = refs[1:]
    if halves is None:
        wbuf, xbuf, kvbuf, queries, sums, largest, totals = refs
    else:
        wq, refs = refs[0], refs[1:]
        nears, fars, refs = refs[: planes - 1], refs[planes - 1 : planes - 1 + halves], refs[planes - 1 + halves :]
        xbuf, kvbuf, queries, sums, largest, totals, wbuf, wsem = refs
        owns = [(wq, aligned(lax.axis_index("seq") & 1, wbuf.shape[1]), slice(None))]
        run_copies(weight_copies(wbuf, wsem, owns, nears, fars, far_order))
    rows_here, width = queries.shape
    here = pl.ds(side * rows_here, rows_here)
    product_loop(tensor_size, sub_size, xbuf.at[:, here, :], wbuf, sums, queries)
    row = lax.broadcasted_iota(jnp.int32, (SEG, SEG), 0)
    causal = row >= lax.broadcasted_iota(jnp.int32, (SEG, SEG), 1)
    for a in range(rows_here // SEG):
        rows = slice(a * SEG, (a + 1) * SEG)
        kvrows = slice(side * rows_here + a * SEG, side * rows_here + (a + 1) * SEG)
        for h in range(width // HD):
            ks, vs = slice(h * HD, (h + 1) * HD), slice(width + h * HD, width + (h + 1) * HD)
            scores = lax.dot_general(queries[rows, ks], kvbuf[kvrows, ks], CONTRACT, preferred_element_type=F32)
            scores = jnp.where(causal, scores * SCALE, -jnp.inf)
            best = jnp.max(scores, axis=1, keepdims=True)
            weights = jnp.exp2(scores - best)
            largest[rows, ks] = jnp.broadcast_to(best, (SEG, HD))
            totals[rows, ks] = jnp.broadcast_to(jnp.sum(weights, axis=1, keepdims=True), (SEG, HD))
            sums[rows, ks] = jnp.dot(weights.astype(BF), kvbuf[kvrows, vs], preferred_element_type=F32)


def attend_local(side, planes, tensor_size, sub_size, turn, weight, far_order, held, kv_tok):
    rows, width = held.shape[1] // 2, kv_tok.shape[1] // 2
    state = [pltpu.VMEM((rows, width), BF)] + [pltpu.VMEM((rows, width), F32)] * 3
    scratch, halves = [], None
    if isinstance(weight, tuple):
        wq, nears, fars = weight
        operands, halves = [wq, *nears, *fars], len(fars)
        specs = [ANY] * len(operands)
        state.append(pltpu.VMEM((wq.shape[0] * planes, width), BF))
        scratch = [pltpu.SemaphoreType.DMA((planes + len(far_order),))]
    else:
        operands, specs = [resident(weight)], [VMEM]
    return pl.pallas_call(
        functools.partial(local_kernel, side, planes, tensor_size, sub_size, far_order, halves),
        out_shape=state,
        in_specs=[SMEM] + specs + [VMEM] * 2,
        out_specs=[VMEM] * len(state),
        scratch_shapes=scratch,
        compiler_params=pltpu.CompilerParams(vmem_limit_bytes=VMEM_LIMIT),
        cost_estimate=cost(4),
        name="attend_local",
    )(turn, *operands, resident(held), resident(kv_tok))


def far_kernel(side, planes, segments, length, queries, sums, largest, totals, *refs):
    mems, (out, membuf, obuf, sems) = refs[: planes // 2], refs[planes // 2 :]
    plane = lax.axis_index("seq")
    rows_here, width = obuf.shape
    slots = rows_here // SEG
    count = mems[0].shape[0]
    copies = []
    for i, mem in enumerate(mems):
        copies.append(pltpu.make_async_copy(mem, membuf.at[pl.ds(i * count, count), :], sems.at[1 + i]))
        copies[-1].start()
    per_plane = count // 2
    mem_total = membuf.shape[0]
    column = lax.broadcasted_iota(jnp.int32, (1, mem_total), 1)
    owner = jnp.zeros((1, mem_total), jnp.int32)
    for distance in range(planes):
        for i in range(slots):
            start = distance * per_plane + i * MEM
            inside = (column >= start) & (column < start + MEM)
            owner = jnp.where(inside, segments[(plane ^ distance) * slots + i], owner)
    position = lax.broadcasted_iota(jnp.int32, (SEG, HD), 0)
    for copy in copies:
        copy.wait()
    for a in range(slots):
        rows = slice(a * SEG, (a + 1) * SEG)
        segment = segments[(plane ^ side) * slots + a]
        allowed = owner < segment
        valid = position + segment * SEG < length[0]
        for h in range(width // HD):
            ks, vs = slice(h * HD, (h + 1) * HD), slice(width + h * HD, width + (h + 1) * HD)
            scores = lax.dot_general(queries[rows, ks], membuf[:, ks], CONTRACT, preferred_element_type=F32)
            scores = jnp.where(allowed, scores * SCALE, -jnp.inf)
            before = largest[rows, ks]
            best = jnp.maximum(before[:, :1], jnp.max(scores, axis=1, keepdims=True))
            weights = jnp.exp2(scores - best)
            factor = jnp.exp2(before - best)
            denominator = totals[rows, ks] * factor + jnp.sum(weights, axis=1, keepdims=True)
            numerator = sums[rows, ks] * factor
            numerator += jnp.dot(weights.astype(BF), membuf[:, vs], preferred_element_type=F32)
            obuf[rows, ks] = jnp.where(valid, numerator / denominator, 0.0).astype(BF)
    dest = out if side else out.at[:, aligned(plane & 1, width)]
    copy = pltpu.make_async_copy(obuf, dest, sems.at[0])
    copy.start()
    copy.wait()


def attend(side, planes, segments, length, state, mems):
    rows, width = state[0].shape
    mem_total = len(mems) * mems[0].shape[0]
    operands = [segments, length, *(resident(value) for value in state), *mems]
    return pl.pallas_call(
        functools.partial(far_kernel, side, planes),
        out_shape=jax.ShapeDtypeStruct((rows, width if side else 2 * width), BF),
        in_specs=[SMEM, SMEM] + [VMEM] * len(state) + [ANY] * len(mems),
        out_specs=ANY,
        scratch_shapes=[
            pltpu.VMEM((mem_total, 2 * width), BF),
            pltpu.VMEM((rows, width), BF),
            pltpu.SemaphoreType.DMA((1 + len(mems),)),
        ],
        compiler_params=pltpu.CompilerParams(vmem_limit_bytes=VMEM_LIMIT),
        cost_estimate=cost(4),
        name="attend",
    )(*operands)


def on_device(
    activations, conv_weight, query_weight, key_weight, value_weight, segment_for_slot, book_length
):
    planes, tensor_size, sub_size = (lax.axis_size(name) for name in ("seq", "tensor", "sub"))
    parity = lax.axis_index("seq") & 1

    kv_same, kv_other, q_same, q_other, q_whole = split_weights(key_weight, value_weight, query_weight)

    def across(block, label):
        return {f"{label}x{k}": (block, "tensor", k) for k in range(1, tensor_size)}

    def within(block, label):
        return {f"{label}c{k}": (block, "sub", k) for k in range(1, sub_size)}

    def distant(distances, name):
        same, other = {"kv": (kv_same, kv_other), "q": (q_same, q_other)}[name]
        return {f"{name}{d}": (other if d & 1 else same, "seq", d) for d in distances}

    def relayed(distances, name):
        return {f"y{name}{d}": (got[f"{name}{d}"], "groups", 1) for d in distances}

    got = {}

    def stage(sends, *computed):
        held = tuple(got[key] for key in fresh)
        new = {}
        for key, (value, axis, distance) in sends.items():
            new[key] = swap(after(value, *held), axis, distance, key)
        ended = lax.optimization_barrier(tuple(new.values()) + computed)
        got.update(zip(new, ended))
        fresh[:] = list(new)
        return ended[len(new) :]

    fresh = []
    every = range(1, planes)
    first = [2] if planes > 2 else []
    second = [d for d in every if d not in first]
    stage(
        {"Xz": (activations, "seq", 1)}
        | across(activations, "A")
        | within(activations, "A0")
        | distant(first, "kv")
    )
    partner = got["Xz"]
    sends = across(partner, "B") | distant(second, "kv") | relayed(first, "kv")
    both = compress(activations, partner, conv_weight)
    hops = {f"C0c{k}": swap(both, "sub", k, f"C0c{k}") for k in range(1, sub_size)}
    both, *ended = stage(sends, both, *hops.values())
    got.update(zip(hops, ended))
    far_planes = range(2, planes)
    second_kv = jnp.concatenate([got[f"kv{d}"] for d in second], axis=0)
    stage(
        distant(far_planes, "q")
        | {"q1": (q_whole, "seq", 1), "ykv": (second_kv, "groups", 1)}
        | across(both, "C")
    )
    sends = within(partner, "B0") | relayed(far_planes, "q")
    for label in ("C", "B", "A"):
        for k in range(1, tensor_size):
            sends |= within(got[f"{label}x{k}"], f"{label}{k}")
    before = tuple(got[key] for key in fresh)
    for key, (value, axis, distance) in sends.items():
        held = before if axis == "groups" else ()
        got[key] = swap(after(value, *held), axis, distance, key)

    def pieces(block, label):
        whole = []
        for k in range(tensor_size):
            whole.append(got[f"{label}x{k}"] if k else block)
            whole += [got[f"{label}{k}c{u}"] for u in range(1, sub_size)]
        return whole

    own_pieces, partner_pieces = pieces(activations, "A"), pieces(partner, "B")
    compressed_pieces = pieces(both, "C")
    sizes = (planes, tensor_size, sub_size)
    kv_parts = ([got[f"kv{d}"] for d in every], [got[f"ykv{d}"] for d in first] + [got["ykv"]], first + second)
    kv_mem, kv_held = project_memory(*sizes, key_weight, value_weight, *kv_parts, compressed_pieces)
    mems = [kv_mem] + [swap(kv_mem, "seq", d, f"m{d}") for d in range(2, planes, 2)]
    kv_tok, held = project_tokens(tensor_size, sub_size, own_pieces, partner_pieces, kv_held)
    q_parts = (query_weight, [got[f"q{d}"] for d in every], [got[f"yq{d}"] for d in far_planes])
    q_order = list(far_planes)
    *state, q_held = attend_local(1, *sizes, segment_for_slot, q_parts, q_order, held, kv_tok)
    theirs = attend(1, planes, segment_for_slot, book_length, state, mems)
    returned = swap(theirs, "seq", 1, "ctx")
    turn = after(segment_for_slot, theirs)
    state = attend_local(0, *sizes, turn, q_held, q_order, held, kv_tok)
    mine = attend(0, planes, segment_for_slot, book_length, state, mems)
    return lax.dynamic_update_slice(mine, returned, (0, (1 - parity) * theirs.shape[1]))


def solution(mesh):
    placed = (
        P(("groups", "seq"), ("tensor", "sub")),
        P(None, ("tensor", "sub")),
        P("seq", ("tensor", "sub")),
        P("seq", ("tensor", "sub")),
        P("seq", ("tensor", "sub")),
        P("groups"),
        P("groups"),
    )
    return jax.shard_map(
        on_device,
        mesh=mesh,
        in_specs=placed,
        out_specs=P(("groups", "seq"), ("tensor", "sub")),
        check_vma=False,
    )
```

```python
import functools
import math

import jax
import jax.numpy as jnp
from jax import lax
from jax.experimental import pallas as pl
from jax.experimental.pallas import tpu as pltpu
from jax.sharding import PartitionSpec as P

HD = 128
CG = 128
RATE = 4
SEG = 256
MEM = 64
BF = jnp.bfloat16


def cost(microseconds):
    return pl.CostEstimate(flops=int(microseconds * 1.0e9), bytes_accessed=1000, transcendentals=0)
F32 = jnp.float32
ANY = pl.BlockSpec(memory_space=pl.ANY)
MEMORY_LIMIT, TOKENS_LIMIT, VMEM_LIMIT = 48 << 20, 38 << 20, 26 << 20
SMEM = pl.BlockSpec(memory_space=pltpu.SMEM)
VMEM = pl.BlockSpec(memory_space=pltpu.VMEM)


EARLY = 2


def swap(value, axis, distance, label):
    size = lax.axis_size(axis)
    with jax.named_scope("L_" + label):
        return lax.ppermute(value, axis, [(i, i ^ distance) for i in range(size)])


def after(value, *others):
    return lax.optimization_barrier((value,) + others)[0]


def resident(value):
    return pltpu.with_memory_space_constraint(value, pltpu.VMEM)


def run_copies(copies):
    for copy in copies:
        copy.start()
    for copy in copies:
        copy.wait()


def aligned(index, size):
    return pl.ds(pl.multiple_of(index * size, size), size)


def split_kernel(wk, wv, wq, kv_same, kv_other, q_same, q_other, q_whole, sems):
    group, parity = lax.axis_index("groups"), lax.axis_index("seq") & 1
    half, width = q_same.shape
    rows = aligned(group, half)
    copies = []
    for target, kv, q in ((parity, kv_same, q_same), (1 - parity, kv_other, q_other)):
        columns = aligned(target, width)
        for source, dest in ((wk, kv.at[:, 0:width]), (wv, kv.at[:, width : 2 * width]), (wq, q)):
            copies.append(pltpu.make_async_copy(source.at[rows, columns], dest, sems.at[len(copies)]))
    source = wq.at[:, aligned(1 - parity, width)]
    copies.append(pltpu.make_async_copy(source, q_whole, sems.at[len(copies)]))
    run_copies(copies)


def split_weights(wk, wv, wq):
    depth, columns = wk.shape
    half, width = depth // 2, columns // 2
    shapes = [(half, 2 * width), (half, 2 * width), (half, width), (half, width), (depth, width)]
    return pl.pallas_call(
        split_kernel,
        out_shape=[jax.ShapeDtypeStruct(s, BF) for s in shapes],
        in_specs=[ANY] * 3,
        out_specs=[VMEM] * 5,
        scratch_shapes=[pltpu.SemaphoreType.DMA((7,))],
        cost_estimate=cost(2),
        name="split_weights",
    )(wk, wv, wq)


def compress_kernel(own_ref, partner_ref, w_ref, out_ref):
    rows, channels = own_ref.shape
    count = rows // RATE
    row = lax.broadcasted_iota(jnp.int32, (count, rows), 0)
    column = lax.broadcasted_iota(jnp.int32, (count, rows), 1)
    taps = []
    for t in range(RATE):
        pick = (column == row * RATE + t).astype(BF)
        pair = [jnp.dot(pick, ref[...], preferred_element_type=F32).astype(BF) for ref in (own_ref, partner_ref)]
        taps.append(jnp.concatenate(pair, axis=0))
    for g in range(channels // CG):
        columns = slice(g * CG, (g + 1) * CG)
        total = jnp.zeros((2 * count, CG), F32)
        for t in range(RATE):
            weight = w_ref[t * CG : (t + 1) * CG, columns]
            total += jnp.dot(taps[t][:, columns], weight, preferred_element_type=F32)
        out_ref[:, columns] = total.astype(BF)


def compress(own, partner, conv_weight):
    count, channels = own.shape
    return pl.pallas_call(
        compress_kernel,
        out_shape=jax.ShapeDtypeStruct((2 * count // RATE, channels), BF),
        in_specs=[VMEM, VMEM, VMEM],
        out_specs=VMEM,
        cost_estimate=cost(5),
        name="compress",
    )(own, partner, conv_weight)


def weight_copies(buffer, sems, owns, nears, fars, far_order):
    plane, group = lax.axis_index("seq"), lax.axis_index("groups")
    depth = owns[0][0].shape[0]
    half = depth // 2
    pieces = [(ref.at[:, columns], aligned(plane, depth), place) for ref, columns, place in owns]
    for distance, near in enumerate(nears, 1):
        if near.shape[0] == depth:
            pieces.append((near, aligned(plane ^ distance, depth), slice(None)))
        else:
            pieces.append((near, aligned((plane ^ distance) * 2 + group, half), slice(None)))
    order = iter(far_order)
    for far in fars:
        for i in range(far.shape[0] // half):
            place = aligned((plane ^ next(order)) * 2 + 1 - group, half)
            pieces.append((far.at[pl.ds(i * half, half), :], place, slice(None)))
    copies = []
    for ref, rows, place in pieces:
        copies.append(pltpu.make_async_copy(ref, buffer.at[rows, place], sems.at[len(copies)]))
    return copies


def block_owner(index, tensor_size, sub_size):
    tensor, sub = lax.axis_index("tensor"), lax.axis_index("sub")
    return (tensor ^ (index // sub_size)) * sub_size + (sub ^ (index % sub_size))


def memory_kernel(planes, tensor_size, sub_size, far_order, halves, *refs):
    blocks = tensor_size * sub_size
    wk, wv = refs[:2]
    nears, fars, refs = refs[2 : planes + 1], refs[planes + 1 : planes + 1 + halves], refs[planes + 1 + halves :]
    pieces, (out, wbuf, xbuf, acc, xsem, wsem) = refs[:blocks], refs[blocks:]
    width = wbuf.shape[1] // 2
    columns = aligned(lax.axis_index("seq") & 1, width)
    owns = [(wk, columns, slice(0, width)), (wv, columns, slice(width, 2 * width))]
    wcopies = weight_copies(wbuf, wsem, owns, nears, fars, far_order)
    xcopies = [pltpu.make_async_copy(pieces[j], xbuf.at[j], xsem.at[j]) for j in range(blocks)]
    for copy in wcopies + xcopies:
        copy.start()
    for copy in wcopies:
        copy.wait()
    product_loop(tensor_size, sub_size, xbuf, wbuf, acc, out, xcopies)


def product_loop(tensor_size, sub_size, xbuf, wbuf, acc, out, waits=()):
    blocks, chunk = xbuf.shape[0], xbuf.shape[2]
    for j in range(blocks):
        if waits:
            waits[j].wait()
        weight = aligned(block_owner(j, tensor_size, sub_size), chunk)
        part = jnp.dot(xbuf[j], wbuf[weight, :], preferred_element_type=F32)
        if j:
            part += acc[...]
        if j < blocks - 1:
            acc[...] = part
        else:
            out[...] = part.astype(BF)


def project_memory(planes, tensor_size, sub_size, wk, wv, nears, fars, far_order, pieces):
    depth, columns = wk.shape
    blocks, (rows, chunk) = len(pieces), pieces[0].shape
    operands = [wk, wv, *nears, *fars, *pieces]
    return pl.pallas_call(
        functools.partial(memory_kernel, planes, tensor_size, sub_size, far_order, len(fars)),
        out_shape=[jax.ShapeDtypeStruct((rows, columns), BF), pltpu.VMEM((depth * planes, columns), BF)],
        in_specs=[ANY] * len(operands),
        out_specs=[VMEM, VMEM],
        scratch_shapes=[
            pltpu.VMEM((blocks, rows, chunk), BF),
            pltpu.VMEM((rows, columns), F32),
            pltpu.SemaphoreType.DMA((blocks,)),
            pltpu.SemaphoreType.DMA((2 + 2 * (planes - 1),)),
        ],
        compiler_params=pltpu.CompilerParams(vmem_limit_bytes=MEMORY_LIMIT),
        cost_estimate=cost(4),
        name="project_memory",
    )(*operands)


def tokens_kernel(tensor_size, sub_size, *refs):
    blocks = tensor_size * sub_size
    pieces, (wbuf, out, xbuf, acc, sems) = refs[: 2 * blocks], refs[2 * blocks :]
    rows, chunk = pieces[0].shape
    copies = []
    for j in range(blocks):
        for side in range(2):
            dest = xbuf.at[j, pl.ds(side * rows, rows), :]
            copies.append(pltpu.make_async_copy(pieces[side * blocks + j], dest, sems.at[len(copies)]))
    for copy in copies:
        copy.start()
    for j in range(blocks):
        weight = aligned(block_owner(j, tensor_size, sub_size), chunk)
        for side in range(2):
            copies[2 * j + side].wait()
            here = slice(side * rows, (side + 1) * rows)
            part = jnp.dot(xbuf[j, here, :], wbuf[weight, :], preferred_element_type=F32)
            if j:
                part += acc[here, :]
            if j < blocks - 1:
                acc[here, :] = part
            else:
                out[here, :] = part.astype(BF)


def project_tokens(tensor_size, sub_size, own, partner, weights):
    blocks, (rows, chunk), columns = len(own), own[0].shape, weights.shape[1]
    return pl.pallas_call(
        functools.partial(tokens_kernel, tensor_size, sub_size),
        out_shape=[pltpu.VMEM((2 * rows, columns), BF), pltpu.VMEM((blocks, 2 * rows, chunk), BF)],
        in_specs=[ANY] * (2 * blocks) + [VMEM],
        out_specs=[VMEM, VMEM],
        scratch_shapes=[pltpu.VMEM((2 * rows, columns), F32), pltpu.SemaphoreType.DMA((2 * blocks,))],
        compiler_params=pltpu.CompilerParams(vmem_limit_bytes=TOKENS_LIMIT),
        cost_estimate=cost(6),
        name="project_tokens",
    )(*own, *partner, resident(weights))


SCALE = HD ** (-0.5) * math.log2(math.e)
CONTRACT = (((1,), (1,)), ((), ()))


def local_kernel(side, planes, tensor_size, sub_size, far_order, halves, *refs):
    refs = refs[1:]
    if halves is None:
        wbuf, xbuf, kvbuf, queries, sums, largest, totals = refs
    else:
        wq, refs = refs[0], refs[1:]
        nears, fars, refs = refs[: planes - 1], refs[planes - 1 : planes - 1 + halves], refs[planes - 1 + halves :]
        xbuf, kvbuf, queries, sums, largest, totals, wbuf, wsem = refs
        owns = [(wq, aligned(lax.axis_index("seq") & 1, wbuf.shape[1]), slice(None))]
        run_copies(weight_copies(wbuf, wsem, owns, nears, fars, far_order))
    rows_here, width = queries.shape
    here = pl.ds(side * rows_here, rows_here)
    product_loop(tensor_size, sub_size, xbuf.at[:, here, :], wbuf, sums, queries)
    row = lax.broadcasted_iota(jnp.int32, (SEG, SEG), 0)
    causal = row >= lax.broadcasted_iota(jnp.int32, (SEG, SEG), 1)
    for a in range(rows_here // SEG):
        rows = slice(a * SEG, (a + 1) * SEG)
        kvrows = slice(side * rows_here + a * SEG, side * rows_here + (a + 1) * SEG)
        for h in range(width // HD):
            ks, vs = slice(h * HD, (h + 1) * HD), slice(width + h * HD, width + (h + 1) * HD)
            scores = lax.dot_general(queries[rows, ks], kvbuf[kvrows, ks], CONTRACT, preferred_element_type=F32)
            scores = jnp.where(causal, scores * SCALE, -jnp.inf)
            best = jnp.max(scores, axis=1, keepdims=True)
            weights = jnp.exp2(scores - best)
            largest[rows, ks] = jnp.broadcast_to(best, (SEG, HD))
            totals[rows, ks] = jnp.broadcast_to(jnp.sum(weights, axis=1, keepdims=True), (SEG, HD))
            sums[rows, ks] = jnp.dot(weights.astype(BF), kvbuf[kvrows, vs], preferred_element_type=F32)


def attend_local(side, planes, tensor_size, sub_size, turn, weight, far_order, held, kv_tok):
    rows, width = held.shape[1] // 2, kv_tok.shape[1] // 2
    state = [pltpu.VMEM((rows, width), BF)] + [pltpu.VMEM((rows, width), F32)] * 3
    scratch, halves = [], None
    if isinstance(weight, tuple):
        wq, nears, fars = weight
        operands, halves = [wq, *nears, *fars], len(fars)
        specs = [ANY] * len(operands)
        state.append(pltpu.VMEM((wq.shape[0] * planes, width), BF))
        scratch = [pltpu.SemaphoreType.DMA((planes + len(far_order),))]
    else:
        operands, specs = [resident(weight)], [VMEM]
    return pl.pallas_call(
        functools.partial(local_kernel, side, planes, tensor_size, sub_size, far_order, halves),
        out_shape=state,
        in_specs=[SMEM] + specs + [VMEM] * 2,
        out_specs=[VMEM] * len(state),
        scratch_shapes=scratch,
        compiler_params=pltpu.CompilerParams(vmem_limit_bytes=VMEM_LIMIT),
        cost_estimate=cost(4),
        name="attend_local",
    )(turn, *operands, resident(held), resident(kv_tok))


def far_kernel(side, planes, segments, length, queries, sums, largest, totals, *refs):
    mems, (out, membuf, obuf, sems) = refs[: planes // 2], refs[planes // 2 :]
    plane = lax.axis_index("seq")
    rows_here, width = obuf.shape
    slots = rows_here // SEG
    count = mems[0].shape[0]
    copies, leaving = [], []
    for i, mem in enumerate(mems):
        copies.append(pltpu.make_async_copy(mem, membuf.at[pl.ds(i * count, count), :], sems.at[i]))
        copies[-1].start()
    per_plane = count // 2
    mem_total = membuf.shape[0]
    column = lax.broadcasted_iota(jnp.int32, (1, mem_total), 1)
    owner = jnp.zeros((1, mem_total), jnp.int32)
    for distance in range(planes):
        for i in range(slots):
            start = distance * per_plane + i * MEM
            inside = (column >= start) & (column < start + MEM)
            owner = jnp.where(inside, segments[(plane ^ distance) * slots + i], owner)
    position = lax.broadcasted_iota(jnp.int32, (SEG, HD), 0)
    for copy in copies:
        copy.wait()
    for a in range(slots):
        rows = slice(a * SEG, (a + 1) * SEG)
        segment = segments[(plane ^ side) * slots + a]
        allowed = owner < segment
        valid = position + segment * SEG < length[0]
        for h in range(width // HD):
            ks, vs = slice(h * HD, (h + 1) * HD), slice(width + h * HD, width + (h + 1) * HD)
            scores = lax.dot_general(queries[rows, ks], membuf[:, ks], CONTRACT, preferred_element_type=F32)
            scores = jnp.where(allowed, scores * SCALE, -jnp.inf)
            before = largest[rows, ks]
            best = jnp.maximum(before[:, :1], jnp.max(scores, axis=1, keepdims=True))
            weights = jnp.exp2(scores - best)
            factor = jnp.exp2(before - best)
            denominator = totals[rows, ks] * factor + jnp.sum(weights, axis=1, keepdims=True)
            numerator = sums[rows, ks] * factor
            numerator += jnp.dot(weights.astype(BF), membuf[:, vs], preferred_element_type=F32)
            obuf[rows, ks] = jnp.where(valid, numerator / denominator, 0.0).astype(BF)
        dest = out.at[rows, :] if side else out.at[rows, aligned(plane & 1, width)]
        leaving.append(pltpu.make_async_copy(obuf.at[rows, :], dest, sems.at[len(mems) + a]))
        leaving[-1].start()
    for copy in leaving:
        copy.wait()


def attend(side, planes, segments, length, state, mems):
    rows, width = state[0].shape
    mem_total = len(mems) * mems[0].shape[0]
    operands = [segments, length, *(resident(value) for value in state), *mems]
    return pl.pallas_call(
        functools.partial(far_kernel, side, planes),
        out_shape=jax.ShapeDtypeStruct((rows, width if side else 2 * width), BF),
        in_specs=[SMEM, SMEM] + [VMEM] * len(state) + [ANY] * len(mems),
        out_specs=ANY,
        scratch_shapes=[
            pltpu.VMEM((mem_total, 2 * width), BF),
            pltpu.VMEM((rows, width), BF),
            pltpu.SemaphoreType.DMA((rows // SEG + len(mems),)),
        ],
        compiler_params=pltpu.CompilerParams(vmem_limit_bytes=VMEM_LIMIT),
        cost_estimate=cost(4),
        name="attend",
    )(*operands)


def on_device(
    activations, conv_weight, query_weight, key_weight, value_weight, segment_for_slot, book_length
):
    planes, tensor_size, sub_size = (lax.axis_size(name) for name in ("seq", "tensor", "sub"))
    parity = lax.axis_index("seq") & 1

    kv_same, kv_other, q_same, q_other, q_whole = split_weights(key_weight, value_weight, query_weight)

    def across(block, label):
        return {f"{label}x{k}": (block, "tensor", k) for k in range(1, tensor_size)}

    def within(block, label):
        return {f"{label}c{k}": (block, "sub", k) for k in range(1, sub_size)}

    def distant(distances, name):
        same, other = {"kv": (kv_same, kv_other), "q": (q_same, q_other)}[name]
        return {f"{name}{d}": (other if d & 1 else same, "seq", d) for d in distances}

    def relayed(distances, name):
        return {f"y{name}{d}": (got[f"{name}{d}"], "groups", 1) for d in distances}

    got = {}

    def stage(sends, *computed):
        held = tuple(got[key] for key in fresh)
        new = {}
        for key, (value, axis, distance) in sends.items():
            new[key] = swap(after(value, *held), axis, distance, key)
        ended = lax.optimization_barrier(tuple(new.values()) + computed)
        got.update(zip(new, ended))
        fresh[:] = list(new)
        return ended[len(new) :]

    fresh = []
    every = range(1, planes)
    first = [2] if planes > 2 else []
    second = [d for d in every[::-1] if d not in first]
    stage(
        {"Xz": (activations, "seq", 1)}
        | across(activations, "A")
        | within(activations, "A0")
        | distant(first, "kv")
    )
    partner = got["Xz"]
    sends = across(partner, "B") | distant(second, "kv") | relayed(first, "kv")
    both = compress(activations, partner, conv_weight)
    hops = {f"C0c{k}": swap(both, "sub", k, f"C0c{k}") for k in range(1, sub_size)}
    both, *ended = stage(sends, both, *hops.values())
    got.update(zip(hops, ended))
    far_planes = range(2, planes)
    second_kv = jnp.concatenate([got[f"kv{d}"] for d in second], axis=0)
    stage(
        distant(far_planes, "q")
        | {"q1": (q_whole, "seq", 1), "ykv": (second_kv, "groups", 1)}
        | across(both, "C")
    )
    sends = within(partner, "B0") | relayed(far_planes, "q")
    for label in ("C", "B", "A"):
        for k in range(1, tensor_size):
            sends |= within(got[f"{label}x{k}"], f"{label}{k}")
    before = tuple(got[key] for key in fresh)
    for key, (value, axis, distance) in sends.items():
        held = before if axis == "groups" else ()
        got[key] = swap(after(value, *held), axis, distance, key)

    def pieces(block, label):
        whole = []
        for k in range(tensor_size):
            whole.append(got[f"{label}x{k}"] if k else block)
            whole += [got[f"{label}{k}c{u}"] for u in range(1, sub_size)]
        return whole

    own_pieces, partner_pieces = pieces(activations, "A"), pieces(partner, "B")
    compressed_pieces = pieces(both, "C")
    sizes = (planes, tensor_size, sub_size)
    kv_parts = ([got[f"kv{d}"] for d in every], [got[f"ykv{d}"] for d in first] + [got["ykv"]], first + second)
    kv_mem, kv_held = project_memory(*sizes, key_weight, value_weight, *kv_parts, compressed_pieces)
    mems = [kv_mem] + [swap(kv_mem, "seq", d, f"m{d}") for d in range(2, planes, 2)]
    kv_tok, held = project_tokens(tensor_size, sub_size, own_pieces, partner_pieces, kv_held)
    q_parts = (query_weight, [got[f"q{d}"] for d in every], [got[f"yq{d}"] for d in far_planes])
    q_order = list(far_planes)
    *state, q_held = attend_local(1, *sizes, segment_for_slot, q_parts, q_order, held, kv_tok)
    theirs = attend(1, planes, segment_for_slot, book_length, state, mems)
    returned = swap(theirs, "seq", 1, "ctx")
    turn = after(segment_for_slot, theirs)
    state = attend_local(0, *sizes, turn, q_held, q_order, held, kv_tok)
    mine = attend(0, planes, segment_for_slot, book_length, state, mems)
    return lax.dynamic_update_slice(mine, returned, (0, (1 - parity) * theirs.shape[1]))


def solution(mesh):
    placed = (
        P(("groups", "seq"), ("tensor", "sub")),
        P(None, ("tensor", "sub")),
        P("seq", ("tensor", "sub")),
        P("seq", ("tensor", "sub")),
        P("seq", ("tensor", "sub")),
        P("groups"),
        P("groups"),
    )
    return jax.shard_map(
        on_device,
        mesh=mesh,
        in_specs=placed,
        out_specs=P(("groups", "seq"), ("tensor", "sub")),
        check_vma=False,
    )
```
